32 devices in a mesh: dp: 4 (over y, x), fsdp: 8 (over z, core).
Axes of the slice: x: 2, y: 2, z: 4, core: 2. Of those that a mesh axis runs over, the one named last changes fastest.
Arguments:
- hidden_in: bfloat16 [6400, 2048], P(('dp', 'fsdp')), may hold values from -6 to 6
- segment_ids: int32 [6400], P(('dp', 'fsdp')), may hold values from 0 to 19, as said below
- parents: int32 [4, 20], P('dp'), may hold values from 0 to 19, as said below
- norm_gain: bfloat16 [2048], P(('dp', 'fsdp')), may hold values from 0.099609375 to 1.8984375
- w_qdown: bfloat16 [2048, 1024], P(('dp', 'fsdp')), may hold values from -0.125 to 0.125
- q_gain: bfloat16 [1024], P(('dp', 'fsdp')), may hold values from 0.099609375 to 1.8984375
- w_qup: bfloat16 [1024, 4096], P(('dp', 'fsdp')), may hold values from -0.375 to 0.375
- w_key: bfloat16 [2048, 256], P(('dp', 'fsdp')), may hold values from -0.125 to 0.125
- w_value: bfloat16 [2048, 256], P(('dp', 'fsdp')), may hold values from -0.125 to 0.125
- w_out: bfloat16 [4096, 2048], P(('dp', 'fsdp')), may hold values from -0.375 to 0.375
- ffn_gain: bfloat16 [2048], P(('dp', 'fsdp')), may hold values from 0.099609375 to 1.8984375
- w_gate: bfloat16 [2048, 5632], P(('dp', 'fsdp')), may hold values from -0.125 to 0.125
- w_up: bfloat16 [2048, 5632], P(('dp', 'fsdp')), may hold values from -0.125 to 0.125
- w_down: bfloat16 [5632, 2048], P(('dp', 'fsdp')), may hold values from -0.15625 to 0.15625
- cotangent: bfloat16 [6400, 2048], P(('dp', 'fsdp')), may hold values from -6 to 6
Outputs:
- layer_out: bfloat16 [6400, 2048], P(('dp', 'fsdp'))
- grad_in: bfloat16 [6400, 2048], P(('dp', 'fsdp'))
- grad_norm_gain: float32 [2048], P(('dp', 'fsdp'))
- grad_w_qdown: float32 [2048, 1024], P(('dp', 'fsdp'))
- grad_q_gain: float32 [1024], P(('dp', 'fsdp'))
- grad_w_qup: float32 [1024, 4096], P(('dp', 'fsdp'))
- grad_w_key: float32 [2048, 256], P(('dp', 'fsdp'))
- grad_w_value: float32 [2048, 256], P(('dp', 'fsdp'))
- grad_w_out: float32 [4096, 2048], P(('dp', 'fsdp'))
- grad_ffn_gain: float32 [2048], P(('dp', 'fsdp'))
- grad_w_gate: float32 [2048, 5632], P(('dp', 'fsdp'))
- grad_w_up: float32 [2048, 5632], P(('dp', 'fsdp'))
- grad_w_down: float32 [5632, 2048], P(('dp', 'fsdp'))
The draws below stay inside these ranges and needn't reach their ends.
Inputs may be any that keep to these rules, and one draw needn't show every extreme that they name: `parents`: each tree has 20 segments: the root, whose parent number is its own, begins a chain of 8 segments; the last of the chain has 4 children, and each of these has 2 children that have none. Segment numbers are a permutation within each tree. `segment_ids`: each tree's tokens form 20 runs of 80 tokens, one segment a run; a segment's run comes after its parent's: the chain first in its order, then the 4 middle segments, then the 8 last ones.
All inputs are finite; a program needn't handle non-finite values.
Results may differ from the reference program's by a relative error of at most 0.025.
Values may be sent and summed in bfloat16 or wider, within the bound.
No kernel may reach another device: no remote copies, remote signals or barrier semaphores. Data moves between devices by JAX's collectives and lax.ppermute only.
A program may use at most 320 MiB of HBM per device.

```python
import jax
import jax.numpy as jnp
from jax import lax

D = 2048
QR = 1024
H = 16
HD = 256
FF = 5632
NSEG = 20
TREE = 1600
SEG = 80
TREES = 4
TOKENS = 6400


def tree_layout(key):

    def one_tree(tree_key):
        label_key, leaf_key = jax.random.split(tree_key)
        labels = jax.random.permutation(label_key, NSEG).astype(jnp.int32)
        owners = jax.random.permutation(leaf_key, jnp.array([0, 0, 1, 1, 2, 2, 3, 3], dtype=jnp.int32))
        parent_slot = jnp.concatenate([jnp.zeros((1,), jnp.int32), jnp.arange(7, dtype=jnp.int32), jnp.full((4,), 7, jnp.int32), 8 + owners])
        parent_labels = jnp.zeros((NSEG,), jnp.int32).at[labels].set(labels[parent_slot])
        return (parent_labels, labels)
    tree_keys = jax.random.split(key, TREES)
    parent_table, slot_labels = jax.vmap(one_tree)(tree_keys)
    tokens = jnp.repeat(slot_labels, SEG, axis=1, total_repeat_length=NSEG * SEG).reshape(TREES * NSEG * SEG)
    return (parent_table, tokens)


def draw_parents(key, part):
    return tree_layout(jax.random.fold_in(key, 11))[0]


def draw_segment_ids(key, part):
    return tree_layout(jax.random.fold_in(key, 11))[1]


def strengthened(values, rng, source, target, blocks, factor):
    owner, partner = [(jnp.arange(values.shape[position]) // (values.shape[position] // blocks)).reshape([-1 if axis == position else 1 for axis in range(values.ndim)]) for position in (source, target)]
    chosen = jax.random.permutation(rng, blocks)[partner]
    strong = (owner == chosen) | (owner == (partner + blocks // 2) % blocks)
    return jnp.where(strong, factor * values, values)


def steps_of(key, extent, pieces, low, largest):
    def one(axis_at, parts):
        steps = jax.random.uniform(jax.random.fold_in(jax.random.fold_in(key, 6), axis_at), (parts,), jnp.float32, low / len(pieces), largest / len(pieces))
        return jnp.repeat(jnp.exp(steps), extent[axis_at] // parts).reshape((-1,) + (1,) * (len(extent) - axis_at - 1))

    factor_of = one(*pieces[0])
    for cut in pieces[1:]:
        factor_of = factor_of * one(*cut)
    return factor_of


def normal_values(key, extent, deviation, most, cuts=(), held_as=jnp.bfloat16):
    entries = jax.random.normal(key, extent, jnp.float32) * deviation
    if len(cuts) > 0:
        entries = steps_of(key, extent, cuts, -0.22, 0.18) * entries
    return jnp.clip(entries, min=-most, max=most).astype(held_as)


def gaussian_with(rng, shape, width, limit, cuts, heavy, kind=jnp.bfloat16):
    entries = width * jax.random.normal(rng, shape, jnp.float32)
    if cuts:
        entries = entries * steps_of(rng, shape, cuts, -0.22, 0.18)
    return jnp.clip(strengthened(entries, jax.random.fold_in(rng, 3), *heavy), -limit, limit).astype(kind)


def setup_inputs(seed: int = 0) -> dict:
    key_of = jax.random.split(jax.random.key(seed), 16)
    return {
        "hidden_in": gaussian_with(key_of[0], (TOKENS, D), 1.0, 6.0, ((0, 32),), (0, 1, 32, 2.75)),
        "segment_ids": draw_segment_ids(jax.random.fold_in(key_of[15], 71), 0),
        "parents": draw_parents(jax.random.fold_in(key_of[15], 71), 0),
        "norm_gain": jnp.clip(1.0 + 0.18 * jax.random.normal(key_of[3], (D,), jnp.float32), 0.099609375, 1.8984375).astype(jnp.bfloat16),
        "w_qdown": normal_values(key_of[4], (D, QR), D ** -0.5, 0.125, ((0, 32),)),
        "q_gain": jnp.clip(1.0 + 0.18 * jax.random.normal(key_of[5], (QR,), jnp.float32), 0.099609375, 1.8984375).astype(jnp.bfloat16),
        "w_qup": normal_values(key_of[6], (QR, H * HD), (QR // 4) ** -0.5, 0.375, ((0, 32),)),
        "w_key": normal_values(key_of[7], (D, HD), D ** -0.5, 0.125, ((0, 32),)),
        "w_value": normal_values(key_of[8], (D, HD), D ** -0.5, 0.125, ((0, 32),)),
        "w_out": normal_values(key_of[9], (H * HD, D), (H * HD // 16) ** -0.5, 0.375, ((0, 32),)),
        "ffn_gain": jnp.clip(1.0 + 0.18 * jax.random.normal(key_of[10], (D,), jnp.float32), 0.099609375, 1.8984375).astype(jnp.bfloat16),
        "w_gate": normal_values(key_of[11], (D, FF), D ** -0.5, 0.125, ((0, 32),)),
        "w_up": normal_values(key_of[12], (D, FF), D ** -0.5, 0.125, ((0, 32),)),
        "w_down": normal_values(key_of[13], (FF, D), (FF // 4) ** -0.5, 0.15625, ((0, 32),)),
        "cotangent": normal_values(key_of[14], (TOKENS, D), 1.0, 6.0, ((0, 32),)),
    }


EPSILON = 1e-06
ROPE_BASE = 10000.0
HIGHEST = lax.Precision.HIGHEST

@jax.custom_vjp
def low(v):
    return lax.optimization_barrier(v.astype(jnp.bfloat16)).astype(jnp.float32)

@jax.custom_vjp
def low_back(v):
    return v

def low_keep(v):
    return (low(v), None)

def low_pass(kept, grad):
    return (grad,)

def back_keep(v):
    return (v, None)

def back_low(kept, grad):
    return (low(grad),)
low.defvjp(low_keep, low_pass)
low_back.defvjp(back_keep, back_low)

def ancestors(parent_row):
    labels = jnp.arange(NSEG, dtype=jnp.int32)

    def climb(step_index, state_pair):
        current, ancestry = state_pair
        current = parent_row[current]
        return (current, jnp.maximum(ancestry, (current[:, None] == labels[None, :]).astype(jnp.float32)))
    start = (labels, (labels[:, None] == labels[None, :]).astype(jnp.float32))
    return lax.fori_loop(0, NSEG - 1, climb, start)[1]

def pick_rows(ancestry, segments):
    return ancestry[segments]

def rotate(values, cosines, sine_table):
    half_width = values.shape[-1] // 2
    first_half = values[..., :half_width]
    second_half = values[..., half_width:]
    return jnp.concatenate([first_half * cosines - second_half * sine_table, second_half * cosines + first_half * sine_table], axis=-1)

def rms_scale(values):
    return lax.rsqrt(lax.optimization_barrier(jnp.mean(values * values, axis=-1, keepdims=True)) + EPSILON)

def block_attention(queries, query_segs, query_anc, query_rows, keys, values, key_segs):
    key_rows = jnp.arange(keys.shape[0], dtype=jnp.int32)
    scores = jnp.einsum('qhd,kd->qhk', queries, keys, precision=HIGHEST) * HD ** (-0.5)
    scores = low_back(scores)
    allowed = (query_anc[:, key_segs] > 0.5) & ((query_segs[:, None] != key_segs[None, :]) | (key_rows[None, :] <= query_rows[:, None]))
    weights = jax.nn.softmax(jnp.where(allowed[:, None, :], scores, -1e+30), axis=-1)
    return jnp.einsum('qhk,kd->qhd', low(weights), values, precision=HIGHEST)

def tree_attention(tree_args):
    queries, keys, values, segments, anc_rows = tree_args
    rows_all = jnp.arange(TREE, dtype=jnp.int32)
    blocked = jax.checkpoint(block_attention)

    def one_block(block_args):
        query_block, seg_block, anc_block, row_block = block_args
        return blocked(query_block, seg_block, anc_block, row_block, keys, values, segments)
    output = lax.map(one_block, (queries.reshape(NSEG, SEG, H, HD), segments.reshape(NSEG, SEG), anc_rows.reshape(NSEG, SEG, NSEG), rows_all.reshape(NSEG, SEG)))
    return output.reshape(TREE, H, HD)

def reference(hidden_in, segment_ids, parents, norm_gain, w_qdown, q_gain, w_qup, w_key, w_value, w_out, ffn_gain, w_gate, w_up, w_down, cotangent):
    tables = jax.vmap(ancestors)(parents)
    seg_depth = lax.optimization_barrier(jnp.sum(tables, axis=2)) - 1.0
    segments = segment_ids.reshape(TREES, TREE)
    token_depth = jnp.take_along_axis(seg_depth, segments, axis=1)
    anc_rows = jax.vmap(pick_rows)(tables, segments)
    offsets = (jnp.arange(TREE, dtype=jnp.int32) % SEG).astype(jnp.float32)
    positions = (token_depth * SEG + offsets[None, :]).reshape(TOKENS)
    inverse = ROPE_BASE ** (-(jnp.arange(HD // 2, dtype=jnp.float32) * 2.0) / HD)
    angles = positions[:, None] * inverse[None, :]
    cosines = jnp.cos(angles)
    sine_table = jnp.sin(angles)

    def layer_forward(inputs, gain_one, down_w, gain_latent, up_w, key_w, value_w, out_w, gain_two, gate_w, upper_w, lower_w):
        normed_in = low(inputs * rms_scale(inputs) * gain_one)
        latent = low_back(jnp.dot(normed_in, down_w, precision=HIGHEST))
        latent_in = low(latent * rms_scale(latent) * gain_latent)
        queries = low_back(jnp.dot(latent_in, up_w, precision=HIGHEST)).reshape(TOKENS, H, HD)
        query_rot = low(rotate(queries, cosines[:, None, :], sine_table[:, None, :]))
        key_rot = low(rotate(low_back(jnp.dot(normed_in, key_w, precision=HIGHEST)), cosines, sine_table))
        values = low(low_back(jnp.dot(normed_in, value_w, precision=HIGHEST)))
        attended = lax.map(tree_attention, (query_rot.reshape(TREES, TREE, H, HD), key_rot.reshape(TREES, TREE, HD), values.reshape(TREES, TREE, HD), segments, anc_rows))
        attended = low(low_back(attended.reshape(TOKENS, H * HD)))
        mixed = inputs + low_back(jnp.dot(attended, out_w, precision=HIGHEST))
        normed_mid = low(mixed * rms_scale(mixed) * gain_two)
        gate_pre = low_back(jnp.dot(normed_mid, gate_w, precision=HIGHEST))
        up_pre = low_back(jnp.dot(normed_mid, upper_w, precision=HIGHEST))
        activated = low(jax.nn.silu(gate_pre) * up_pre)
        return mixed + low_back(jnp.dot(activated, lower_w, precision=HIGHEST))
    result, pullback = jax.vjp(layer_forward, hidden_in.astype(jnp.float32), norm_gain.astype(jnp.float32), w_qdown.astype(jnp.float32), q_gain.astype(jnp.float32), w_qup.astype(jnp.float32), w_key.astype(jnp.float32), w_value.astype(jnp.float32), w_out.astype(jnp.float32), ffn_gain.astype(jnp.float32), w_gate.astype(jnp.float32), w_up.astype(jnp.float32), w_down.astype(jnp.float32))
    gradients = pullback(cotangent.astype(jnp.float32))
    return (result.astype(jnp.bfloat16), gradients[0].astype(jnp.bfloat16), gradients[1], gradients[2], gradients[3], gradients[4], gradients[5], gradients[6], gradients[7], gradients[8], gradients[9], gradients[10], gradients[11])
```

```python
import functools

import jax
import jax.numpy as jnp
from jax import lax
from jax.experimental import pallas as pl
from jax.experimental.pallas import tpu as pltpu
from jax.sharding import PartitionSpec as P

H = 16
HD = 256
NSEG = 20

EPSILON = 1e-06
ROPE_BASE = 10000.0
HIGHEST = lax.Precision.HIGHEST
NEGATIVE = -1e30
BF = jnp.bfloat16
F32 = jnp.float32
CHUNK = 160
TREE = ("q", "r", "c")
LINE = ("q", "r")
SHARE = ("r", "c")
VMEM_LIMIT = 48 * 1024 * 1024


def dot32(a, b):
    return jnp.dot(a, b, preferred_element_type=F32)


def dot_nt(a, b):
    return lax.dot_general(a, b, (((1,), (1,)), ((), ())), preferred_element_type=F32)


def dot_tn(a, b):
    return lax.dot_general(a, b, (((0,), (0,)), ((), ())), preferred_element_type=F32)


def rms_scale(values):
    return lax.rsqrt(jnp.mean(values * values, axis=-1, keepdims=True) + EPSILON)


def norm_back(upstream, normed, row_scale, gain_vec):
    scaled = upstream * gain_vec
    inner_mean = jnp.mean(scaled * normed, axis=-1, keepdims=True)
    return (row_scale * (scaled - normed * inner_mean), jnp.sum(upstream * normed, axis=0))


def rotate(values, cosines, sines):
    half = values.shape[-1] // 2
    a, b = values[..., :half], values[..., half:]
    return jnp.concatenate([a * cosines - b * sines, b * cosines + a * sines], axis=-1)


def tile_plan(tile, chunks_per_tile):
    count = jnp.where(tile == 4, 4, tile + 1) * chunks_per_tile
    return count


def chunk_start(tile, j, chunks_per_tile):
    jump = jnp.where((tile == 4) & (j >= 3 * chunks_per_tile), chunks_per_tile, 0)
    return (j + jump) * CHUNK


def seen(k0, bits_row, tile_rows, q0, heads, seg_len):
    shape = (CHUNK, heads * tile_rows)
    key_pos = lax.broadcasted_iota(jnp.int32, (CHUNK, 1), 0) + k0
    key_bit = jnp.left_shift(jnp.int32(1), key_pos // seg_len)
    lane = lax.broadcasted_iota(jnp.int32, (1, heads * tile_rows), 1)
    q_pos = q0 + lax.rem(lane, tile_rows)
    reach = jnp.broadcast_to(key_bit, shape) & jnp.broadcast_to(bits_row, shape)
    return (reach != 0) & (jnp.broadcast_to(key_pos, shape) <= jnp.broadcast_to(q_pos, shape))


def attn_fwd_kernel(heads, seg_len, bits_ref, q_ref, k_ref, v_ref, att_ref, lse_ref, qs, st):
    tile_rows = 4 * seg_len
    width = heads * tile_rows
    per_tile = tile_rows // CHUNK
    scale = HD ** (-0.5)

    def one_tile(tile, carry):
        q0 = pl.multiple_of(tile * tile_rows, tile_rows)
        for h in range(heads):
            qs[h * tile_rows : (h + 1) * tile_rows, :] = q_ref[pl.ds(q0, tile_rows), h * HD : (h + 1) * HD]
        bits_row = bits_ref[tile]
        n_chunks = tile_plan(tile, per_tile)

        def score(j, top):
            k0 = pl.multiple_of(chunk_start(tile, j, per_tile), CHUNK)
            s = dot_nt(k_ref[pl.ds(k0, CHUNK), :], qs[...]) * scale
            s = jnp.where(seen(k0, bits_row, tile_rows, q0, heads, seg_len), s, NEGATIVE)
            st[pl.ds(pl.multiple_of(j * CHUNK, CHUNK), CHUNK), :] = s
            return jnp.maximum(top, jnp.max(s, axis=0, keepdims=True))

        top = lax.fori_loop(0, n_chunks, score, jnp.full((1, width), NEGATIVE, F32))

        def expo(j, total):
            at = pl.ds(pl.multiple_of(j * CHUNK, CHUNK), CHUNK)
            p = jnp.exp(st[at, :] - top)
            st[at, :] = p
            return total + jnp.sum(p, axis=0, keepdims=True)

        total = lax.fori_loop(0, n_chunks, expo, jnp.zeros((1, width), F32))
        inv = 1.0 / total
        lse_ref[tile] = top + jnp.log(total)

        def gather(j, acc):
            k0 = pl.multiple_of(chunk_start(tile, j, per_tile), CHUNK)
            at = pl.ds(pl.multiple_of(j * CHUNK, CHUNK), CHUNK)
            probs = (st[at, :] * inv).astype(BF)
            return acc + dot_tn(v_ref[pl.ds(k0, CHUNK), :], probs)

        out = lax.fori_loop(0, n_chunks, gather, jnp.zeros((HD, width), F32))
        out = out.T.astype(BF)
        for h in range(heads):
            att_ref[pl.ds(q0, tile_rows), h * HD : (h + 1) * HD] = out[h * tile_rows : (h + 1) * tile_rows, :]
        return carry

    lax.fori_loop(0, 5, one_tile, 0)


def attn_bwd_kernel(
    heads, seg_len, bits_ref, lse_ref, cos_ref, sin_ref, q_ref, k_ref, v_ref, da_ref, dq_ref, dk_ref, dv_ref, qs, das, pt, dpt, dk, dv
):
    tile_rows = 4 * seg_len
    width = heads * tile_rows
    per_tile = tile_rows // CHUNK
    scale = HD ** (-0.5)
    dk[...] = jnp.zeros_like(dk)
    dv[...] = jnp.zeros_like(dv)

    def one_tile(tile, carry):
        q0 = pl.multiple_of(tile * tile_rows, tile_rows)
        for h in range(heads):
            rows = slice(h * tile_rows, (h + 1) * tile_rows)
            cols = slice(h * HD, (h + 1) * HD)
            qs[rows, :] = q_ref[pl.ds(q0, tile_rows), cols]
            das[rows, :] = da_ref[pl.ds(q0, tile_rows), cols]
        bits_row = bits_ref[tile]
        lse_row = lse_ref[tile]
        n_chunks = tile_plan(tile, per_tile)

        def first(j, delta):
            k0 = pl.multiple_of(chunk_start(tile, j, per_tile), CHUNK)
            at = pl.ds(pl.multiple_of(j * CHUNK, CHUNK), CHUNK)
            s = dot_nt(k_ref[pl.ds(k0, CHUNK), :], qs[...]) * scale
            p = jnp.where(seen(k0, bits_row, tile_rows, q0, heads, seg_len), jnp.exp(s - lse_row), 0.0)
            low = p.astype(BF)
            dp = dot_nt(v_ref[pl.ds(k0, CHUNK), :], das[...])
            pt[at, :] = p
            dpt[at, :] = dp
            dv[pl.ds(k0, CHUNK), :] += dot32(low, das[...])
            return delta + jnp.sum(low.astype(F32) * dp, axis=0, keepdims=True)

        delta = lax.fori_loop(0, n_chunks, first, jnp.zeros((1, width), F32))

        def second(j, acc):
            k0 = pl.multiple_of(chunk_start(tile, j, per_tile), CHUNK)
            at = pl.ds(pl.multiple_of(j * CHUNK, CHUNK), CHUNK)
            ds = (pt[at, :] * (dpt[at, :] - delta)).astype(BF)
            dk[pl.ds(k0, CHUNK), :] += dot32(ds, qs[...])
            return acc + dot_tn(k_ref[pl.ds(k0, CHUNK), :], ds)

        acc = lax.fori_loop(0, n_chunks, second, jnp.zeros((HD, width), F32))
        out = (acc * scale).T
        at = pl.ds(q0, tile_rows)
        for h in range(heads):
            grad = out[h * tile_rows : (h + 1) * tile_rows, :]
            dq_ref[at, h * HD : (h + 1) * HD] = rotate(grad, cos_ref[at, :], -sin_ref[at, :]).astype(BF)
        return carry

    lax.fori_loop(0, 5, one_tile, 0)
    dk_ref[...] = (dk[...] * scale).astype(BF)
    dv_ref[...] = dv[...].astype(BF)


def attention(bits, q, k, v, heads, seg_len):
    tree_len = q.shape[0]
    width = heads * 4 * seg_len
    work = heads * tree_len * tree_len // 2
    return pl.pallas_call(
        functools.partial(attn_fwd_kernel, heads, seg_len),
        out_shape=(
            jax.ShapeDtypeStruct((tree_len, heads * HD), BF),
            jax.ShapeDtypeStruct((5, 1, width), F32),
        ),
        in_specs=[pl.BlockSpec(memory_space=pltpu.VMEM)] * 4,
        out_specs=(pl.BlockSpec(memory_space=pltpu.VMEM),) * 2,
        scratch_shapes=[pltpu.VMEM((width, HD), BF), pltpu.VMEM((16 * seg_len, width), F32)],
        compiler_params=pltpu.CompilerParams(vmem_limit_bytes=VMEM_LIMIT),
        cost_estimate=pl.CostEstimate(flops=4 * HD * work, bytes_accessed=6 * tree_len * HD * 2, transcendentals=work),
        name="attn_fwd",
    )(bits, q, k, v)


def attention_back(bits, lse, cosines, sines, q, k, v, da, heads, seg_len):
    tree_len = q.shape[0]
    width = heads * 4 * seg_len
    work = heads * tree_len * tree_len // 2
    return pl.pallas_call(
        functools.partial(attn_bwd_kernel, heads, seg_len),
        out_shape=(
            jax.ShapeDtypeStruct((tree_len, heads * HD), BF),
            jax.ShapeDtypeStruct((tree_len, HD), BF),
            jax.ShapeDtypeStruct((tree_len, HD), BF),
        ),
        in_specs=[pl.BlockSpec(memory_space=pltpu.VMEM)] * 8,
        out_specs=(pl.BlockSpec(memory_space=pltpu.VMEM),) * 3,
        scratch_shapes=[
            pltpu.VMEM((width, HD), BF),
            pltpu.VMEM((width, HD), BF),
            pltpu.VMEM((16 * seg_len, width), F32),
            pltpu.VMEM((16 * seg_len, width), F32),
            pltpu.VMEM((tree_len, HD), F32),
            pltpu.VMEM((tree_len, HD), F32),
        ],
        compiler_params=pltpu.CompilerParams(vmem_limit_bytes=VMEM_LIMIT),
        cost_estimate=pl.CostEstimate(flops=10 * HD * work, bytes_accessed=12 * tree_len * HD * 2, transcendentals=work),
        name="attn_bwd",
    )(bits, lse, cosines, sines, q, k, v, da)


def body(
    hidden_in,
    segment_ids,
    parents,
    norm_gain,
    w_qdown,
    q_gain,
    w_qup,
    w_key,
    w_value,
    w_out,
    ffn_gain,
    w_gate,
    w_up,
    w_down,
    cotangent,
):
    rows, model = hidden_in.shape
    dn, cn = lax.axis_size("dp"), lax.axis_size("c")
    zn, sn = lax.axis_size(LINE), lax.axis_size(SHARE)
    fn = lax.axis_size(TREE)
    heads = H // fn
    latent_width = w_qdown.shape[1]
    in_width = latent_width + 2 * HD
    per_row, per_latent = norm_gain.shape[0], q_gain.shape[0]
    d_at, c_at, f_at = lax.axis_index("dp"), lax.axis_index("c"), lax.axis_index(TREE)
    tree_len = rows * fn
    seg_len = tree_len // NSEG

    def exchange(parts, axes):
        return lax.all_to_all(parts, axes, split_axis=0, concat_axis=0, tiled=True)

    def spread(block, axes):
        return exchange(jnp.broadcast_to(block[None], (lax.axis_size(axes),) + block.shape), axes)

    def total(parts, axes):
        return jnp.sum(exchange(parts.astype(BF), axes).astype(F32), axis=0)

    def other_core(a):
        return lax.ppermute(a, "c", [(c, (c + 1) % cn) for c in range(cn)])

    def by_core(mine, axis):
        came = other_core(mine)
        return jnp.stack([jnp.where(c_at == 0, mine, came), jnp.where(c_at == 0, came, mine)], axis=axis)

    def at_index(a, index, axis=0):
        return lax.dynamic_index_in_dim(a, index, axis, keepdims=False)

    def after(a, *before):
        return lax.optimization_barrier((a,) + before)[0]

    def own_rows(a):
        return lax.dynamic_slice_in_dim(a, f_at * rows, rows, 0)

    def tree_gather(block):
        return lax.all_gather(block, TREE, axis=0, tiled=True)

    def tree_scatter(parts):
        return lax.psum_scatter(parts, TREE, scatter_dimension=0, tiled=True).astype(F32)

    def over_dp(a, m):
        return lax.ppermute(a, "dp", [(d, d ^ m) for d in range(dn)])

    def spread_dp(block):
        out = jnp.zeros((dn,) + block.shape, block.dtype)
        for m in range(dn):
            got = over_dp(block, m) if m else block
            out = lax.dynamic_update_index_in_dim(out, got, d_at ^ m, 0)
        return out

    tags = -(-rows // per_row)
    extra = jnp.concatenate(
        [
            norm_gain[:, None],
            ffn_gain[:, None],
            jnp.pad(q_gain, (0, per_row - per_latent))[:, None],
            jnp.pad(segment_ids.astype(BF), (0, tags * per_row - rows)).reshape(tags, per_row).T,
            jnp.zeros((per_row, 125 - tags), BF),
        ],
        axis=1,
    )
    x_all = tree_gather(hidden_in)
    in_block = jnp.concatenate([w_qdown, w_key, w_value, extra], axis=1)
    in_mine = spread(spread(in_block, LINE), "dp")
    in_full = by_core(in_mine, 2).reshape(model, in_width + 128)
    w_in = in_full[:, :in_width]
    extra = in_full[:, in_width:].T.astype(F32)
    gain_one, gain_two = extra[0], extra[1]
    gain_latent = extra[2].reshape(dn * fn, per_row)[:, :per_latent].reshape(latent_width)
    run_labels = lax.dynamic_slice_in_dim(extra[3 : 3 + tags].reshape(tags, dn, fn, per_row), d_at, 1, 1)[:, 0]
    run_labels = jnp.swapaxes(run_labels, 0, 1).reshape(fn, tags * per_row)[:, :rows]
    run_labels = run_labels.reshape(tree_len)[::seg_len].astype(jnp.int32)

    qup_rows, out_rows = w_qup.shape[0], w_out.shape[0]
    qn = fn // sn
    qup_cols = jnp.transpose(w_qup.reshape(qup_rows, sn, heads, qn, HD), (3, 1, 0, 2, 4))
    qup_cols = exchange(after(qup_cols.reshape(fn, qup_rows, heads * HD), in_mine), TREE)
    qup_cols = spread_dp(qup_cols).reshape(latent_width, heads * HD)
    out_cols = exchange(spread_dp(after(w_out, in_mine)).reshape(sn, heads, out_rows, model), SHARE)
    out_cols = jnp.swapaxes(out_cols, 0, 1).reshape(heads * HD, model)
    cot = tree_gather(after(cotangent, x_all))

    labels = jnp.arange(NSEG, dtype=jnp.int32)
    reach = jnp.maximum(
        (labels[:, None] == labels[None, :]).astype(F32), (parents[0][:, None] == labels[None, :]).astype(F32)
    )
    for _ in range(5):
        reach = jnp.minimum(jnp.dot(reach, reach, precision=HIGHEST), 1.0)
    pick_run = (run_labels[:, None] == labels[None, :]).astype(F32)
    run_reach = jnp.dot(jnp.dot(pick_run, reach, precision=HIGHEST), pick_run.T, precision=HIGHEST)
    run_depth = jnp.sum(run_reach, axis=1) - 1.0
    run_bits = jnp.sum(jnp.where(run_reach > 0.5, jnp.left_shift(1, labels)[None, :], 0), axis=1).astype(jnp.int32)
    bits = jnp.broadcast_to(run_bits.reshape(5, 1, 4, 1), (5, heads, 4, seg_len)).reshape(5, 1, heads * 4 * seg_len)
    inverse = ROPE_BASE ** (-(jnp.arange(HD // 2, dtype=F32) * 2.0) / HD)
    coarse = (run_depth * seg_len)[:, None] * inverse[None, :]
    fine = jnp.arange(seg_len, dtype=F32)[:, None] * inverse[None, :]
    cos_a, sin_a = jnp.cos(coarse)[:, None, :], jnp.sin(coarse)[:, None, :]
    cos_b, sin_b = jnp.cos(fine)[None, :, :], jnp.sin(fine)[None, :, :]
    cosines = (cos_a * cos_b - sin_a * sin_b).reshape(tree_len, HD // 2)
    sines = (sin_a * cos_b + cos_a * sin_b).reshape(tree_len, HD // 2)

    unit_rows = w_down.shape[0]
    units = dn * unit_rows

    def unit_columns(weight):
        return jnp.transpose(weight.reshape(per_row, dn, fn, unit_rows), (2, 0, 1, 3)).reshape(fn, 1, per_row, units)

    unit_cols = jnp.concatenate([unit_columns(w_gate), unit_columns(w_up)], axis=1)
    unit_cols = exchange(after(unit_cols, x_all, qup_cols), TREE)

    x_wide = x_all.astype(F32)
    normed_all = (x_wide * rms_scale(x_wide) * gain_one).astype(BF)
    mixed_in = dot32(normed_all, w_in)
    latent_all = mixed_in[:, :latent_width]
    latent_in = (latent_all * rms_scale(latent_all) * gain_latent).astype(BF)
    key_all = rotate(mixed_in[:, latent_width : latent_width + HD], cosines, sines).astype(BF)
    value_all = mixed_in[:, latent_width + HD :].astype(BF)
    query_wide = dot32(latent_in, qup_cols)
    query_all = jnp.concatenate(
        [rotate(query_wide[:, h * HD : (h + 1) * HD], cosines, sines).astype(BF) for h in range(heads)], axis=1
    )
    attended, lse = attention(bits, query_all, key_all, value_all, heads, seg_len)
    x = hidden_in.astype(F32)
    out_part = dot32(after(attended, unit_cols, cot), out_cols).astype(BF)
    unit_cols = spread(after(unit_cols, out_part), "dp")
    mixed = x + after(tree_scatter(out_part), unit_cols)
    gate_cols = unit_cols[:, :, 0].reshape(model, units)
    up_cols = unit_cols[:, :, 1].reshape(model, units)

    scale_two = rms_scale(mixed)
    normed_two = mixed * scale_two
    normed_mid = (normed_two * gain_two).astype(BF)
    down_rows = spread(after(w_down, normed_mid), "dp").reshape(units, model)
    mid = after(tree_gather(normed_mid), down_rows, gate_cols, up_cols)
    gate = dot32(mid, gate_cols)
    up = dot32(mid, up_cols)
    sig = jax.nn.sigmoid(gate)
    activated = (gate * sig * up).astype(BF)
    act_grad = dot_nt(cot, down_rows)
    gate_grad = (act_grad * up * sig * (1.0 + gate * (1.0 - sig))).astype(BF)
    up_grad = (act_grad * gate * sig).astype(BF)
    mid_part = (dot_nt(gate_grad, gate_cols) + dot_nt(up_grad, up_cols)).astype(BF)
    down_parts = dot_tn(after(activated, mid_part), cot).astype(BF).reshape(dn, unit_rows, model)
    grad_down = total(down_parts, "dp")
    mid_late = after(mid, mid_part)
    unit_parts = jnp.stack(
        [dot_tn(mid_late, gate_grad).astype(BF).reshape(dn, fn * per_row, units),
         dot_tn(mid_late, up_grad).astype(BF).reshape(dn, fn * per_row, units)], axis=1
    )
    mid_grad = after(tree_scatter(mid_part), unit_parts, grad_down)
    mixed_back, gain_two_part = norm_back(mid_grad, normed_two, scale_two, gain_two)
    mixed_grad = cotangent.astype(F32) + mixed_back
    branch_grad = mixed_grad.astype(BF)

    unit_own = total(after(unit_parts, branch_grad), "dp").astype(BF).reshape(2, fn, per_row, units)
    branch = after(tree_gather(branch_grad), unit_own)
    unit_own = exchange(after(jnp.swapaxes(unit_own, 0, 1), branch), TREE).reshape(fn, 2, per_row, dn, unit_rows)
    attended_grad = dot_nt(branch, out_cols).astype(BF)
    query_grad, key_part, value_part = attention_back(
        bits, lse, cosines, sines, query_all, key_all, value_all, attended_grad, heads, seg_len
    )
    latent_part = dot_nt(query_grad, qup_cols).astype(BF)
    back_part = after(jnp.concatenate([latent_part, key_part, value_part], axis=1), unit_own)
    out_grads = jnp.swapaxes(
        dot_tn(attended, after(branch, back_part)).astype(BF).reshape(heads, sn, out_rows, model), 0, 1
    )
    grad_out = total(exchange(out_grads, SHARE).reshape(dn, out_rows, model), "dp")
    grad_qup = dot_tn(latent_in, after(query_grad, back_part))
    grad_qup = total(grad_qup.reshape(dn, fn * qup_rows, heads * HD), "dp").astype(BF)
    back = after(tree_scatter(back_part), grad_qup, grad_out)
    layer_part = dot32(after(activated, back_part), down_rows).astype(BF)
    layer_out = (mixed + tree_scatter(after(layer_part, back))).astype(BF)
    grad_qup = exchange(grad_qup.reshape(fn, qup_rows, heads * HD), TREE).reshape(qn, sn, qup_rows, heads, HD)
    grad_qup = jnp.transpose(grad_qup, (2, 1, 3, 0, 4)).reshape(qup_rows, H * HD).astype(F32)
    unit_own = jnp.transpose(unit_own, (1, 2, 3, 0, 4)).reshape(2, per_row, dn * fn * unit_rows).astype(F32)

    scale_one = rms_scale(x)
    normed_one = x * scale_one
    normed_in = (normed_one * gain_one).astype(BF)
    latent = own_rows(latent_all)
    scale_latent = rms_scale(latent)
    latent_back, gain_latent_part = norm_back(
        back[:, :latent_width], latent * scale_latent, scale_latent, gain_latent
    )
    key_grad = rotate(back[:, latent_width : latent_width + HD], own_rows(cosines), -own_rows(sines))
    in_grad = jnp.concatenate([latent_back, key_grad, back[:, latent_width + HD :]], axis=1).astype(BF)
    normed_grad = dot_nt(in_grad, w_in)
    input_back, gain_one_part = norm_back(normed_grad, normed_one, scale_one, gain_one)
    grad_in = (mixed_grad + input_back).astype(BF)

    def per_core(a, core):
        return at_index(a.reshape(a.shape[0], dn * zn, cn, per_row), core, 2).reshape(a.shape[0], dn * zn * per_row)

    def over_cores(sent, kept):
        return other_core(sent.astype(BF)).astype(F32) + kept

    in_own = over_cores(dot_tn(per_core(normed_in, 1 - c_at), in_grad), dot_tn(per_core(normed_in, c_at), in_grad))

    def per_device(a):
        return jnp.pad(a.reshape(dn * fn, -1), ((0, 0), (0, per_row - a.shape[0] // (dn * fn)))).reshape(1, model)

    gain_parts = jnp.concatenate([per_device(a) for a in (gain_one_part, gain_two_part, gain_latent_part)], axis=0)
    gain_parts = jnp.pad(gain_parts, ((0, 125), (0, 0)))
    gain_own = over_cores(per_core(gain_parts, 1 - c_at), per_core(gain_parts, c_at)).T
    in_own = jnp.concatenate([in_own, gain_own], axis=1).reshape(dn, zn, per_row, in_width + 128)
    in_sum = total(total(in_own, "dp"), LINE)
    return (
        layer_out,
        grad_in,
        in_sum[:, in_width],
        in_sum[:, :latent_width],
        in_sum[:per_latent, in_width + 2],
        grad_qup,
        in_sum[:, latent_width : latent_width + HD],
        in_sum[:, latent_width + HD : in_width],
        grad_out,
        in_sum[:, in_width + 1],
        unit_own[0],
        unit_own[1],
        grad_down,
    )


def solution(mesh):
    dn, fn = mesh.shape["dp"], mesh.shape["fsdp"]
    share = dn * fn // H
    fine = jax.sharding.Mesh(mesh.devices.reshape(dn, fn // share, share // 2, 2), ("dp",) + TREE)
    split = P(("dp",) + TREE, None)
    line = P(("dp",) + TREE)
    placed = (
        split, line, P("dp", None), line, split, line, split, split, split, split, line, split, split, split, split,
    )
    given = (split, split, line, split, line, split, split, split, split, line, split, split, split)
    return jax.shard_map(body, mesh=fine, in_specs=placed, out_specs=given, check_vma=False)
```

```python
import functools

import jax
import jax.numpy as jnp
from jax import lax
from jax.experimental import pallas as pl
from jax.experimental.layout import Layout, with_layout_constraint
from jax.experimental.pallas import tpu as pltpu
from jax.sharding import PartitionSpec as P

H = 16
HD = 256
NSEG = 20

EPSILON = 1e-06
ROPE_BASE = 10000.0
HIGHEST = lax.Precision.HIGHEST
NEGATIVE = -1e30
BF = jnp.bfloat16
F32 = jnp.float32
CHUNK = 160
TREE = ("q", "r", "c")
LINE = ("q", "r")
SHARE = ("r", "c")
VMEM_LIMIT = 48 * 1024 * 1024


def dot32(a, b):
    return jnp.dot(a, b, preferred_element_type=F32)


def dot_nt(a, b):
    return lax.dot_general(a, b, (((1,), (1,)), ((), ())), preferred_element_type=F32)


def dot_tn(a, b):
    return lax.dot_general(a, b, (((0,), (0,)), ((), ())), preferred_element_type=F32)


def rms_scale(values):
    return lax.rsqrt(jnp.mean(values * values, axis=-1, keepdims=True) + EPSILON)


def norm_back(upstream, normed, row_scale, gain_vec):
    scaled = upstream * gain_vec
    inner_mean = jnp.mean(scaled * normed, axis=-1, keepdims=True)
    return row_scale * (scaled - normed * inner_mean)


def gain_column(upstream, normed, column):
    picked = (lax.broadcasted_iota(jnp.int32, (upstream.shape[0], 128), 1) == column).astype(F32)
    return lax.dot_general(
        upstream * normed, picked, (((0,), (0,)), ((), ())), precision=HIGHEST, preferred_element_type=F32
    )


def rotate(values, cosines, sines):
    half = values.shape[-1] // 2
    a, b = values[..., :half], values[..., half:]
    return jnp.concatenate([a * cosines - b * sines, b * cosines + a * sines], axis=-1)


def tile_plan(tile, per_tile):
    free = jnp.minimum(tile, 2) * per_tile
    count = jnp.where(tile == 4, 4, tile + 1) * per_tile
    return free, count


def chunk_start(tile, j, per_tile):
    jump = jnp.where((tile == 4) & (j >= 3 * per_tile), per_tile, 0)
    return pl.multiple_of((j + jump) * CHUNK, CHUNK)


def seen(k0, bits_row, q_pos, seg_len):
    shape = (CHUNK, q_pos.shape[1])
    key_pos = lax.broadcasted_iota(jnp.int32, (CHUNK, 1), 0) + k0
    key_bit = jnp.left_shift(jnp.int32(1), key_pos // seg_len)
    reach = jnp.broadcast_to(key_bit, shape) & jnp.broadcast_to(bits_row, shape)
    return (reach != 0) & (jnp.broadcast_to(key_pos, shape) <= jnp.broadcast_to(q_pos, shape))


def query_places(tile, tile_rows, heads):
    lane = lax.broadcasted_iota(jnp.int32, (1, heads * tile_rows), 1)
    return tile * tile_rows + lax.rem(lane, tile_rows)


def attn_fwd_kernel(heads, seg_len, bits_ref, q_ref, k_ref, v_ref, att_ref, lse_ref, qs, st):
    tile_rows = 4 * seg_len
    width = heads * tile_rows
    per_tile = tile_rows // CHUNK
    scale = HD ** (-0.5)

    def one_tile(tile, carry):
        q0 = pl.multiple_of(tile * tile_rows, tile_rows)
        for h in range(heads):
            rows = q_ref[pl.ds(q0, tile_rows), h * HD : (h + 1) * HD]
            qs[h * tile_rows : (h + 1) * tile_rows, :] = (rows.astype(F32) * scale).astype(BF)
        bits_row = bits_ref[tile]
        q_pos = query_places(tile, tile_rows, heads)
        free, count = tile_plan(tile, per_tile)

        def score(masked, j, top):
            k0 = chunk_start(tile, j, per_tile)
            s = dot_nt(k_ref[pl.ds(k0, CHUNK), :], qs[...])
            if masked:
                s = jnp.where(seen(k0, bits_row, q_pos, seg_len), s, NEGATIVE)
            st[pl.ds(pl.multiple_of(j * CHUNK, CHUNK), CHUNK), :] = s
            return jnp.maximum(top, jnp.max(s, axis=0, keepdims=True))

        top = lax.fori_loop(0, free, functools.partial(score, False), jnp.full((1, width), NEGATIVE, F32))
        top = lax.fori_loop(free, count, functools.partial(score, True), top)

        def gather(j, carry):
            total, acc = carry
            k0 = chunk_start(tile, j, per_tile)
            p = jnp.exp(st[pl.ds(pl.multiple_of(j * CHUNK, CHUNK), CHUNK), :] - top)
            acc = acc + dot_tn(v_ref[pl.ds(k0, CHUNK), :], p.astype(BF))
            return total + jnp.sum(p, axis=0, keepdims=True), acc

        total, out = lax.fori_loop(0, count, gather, (jnp.zeros((1, width), F32), jnp.zeros((HD, width), F32)))
        lse_ref[tile] = top + jnp.log(total)
        out = (out * (1.0 / total)).T.astype(BF)
        for h in range(heads):
            att_ref[pl.ds(q0, tile_rows), h * HD : (h + 1) * HD] = out[h * tile_rows : (h + 1) * tile_rows, :]
        return carry

    lax.fori_loop(0, 5, one_tile, 0)


def attn_bwd_kernel(
    heads, seg_len, bits_ref, lse_ref, cos_ref, sin_ref, q_ref, k_ref, v_ref, att_ref, da_ref,
    dq_ref, dk_ref, dv_ref, qs, das, dk, dv,
):
    tile_rows = 4 * seg_len
    width = heads * tile_rows
    per_tile = tile_rows // CHUNK
    scale = HD ** (-0.5)
    dk[...] = jnp.zeros_like(dk)
    dv[...] = jnp.zeros_like(dv)

    def one_tile(tile, carry):
        q0 = pl.multiple_of(tile * tile_rows, tile_rows)
        deltas = []
        for h in range(heads):
            rows = slice(h * tile_rows, (h + 1) * tile_rows)
            cols = slice(h * HD, (h + 1) * HD)
            here = pl.ds(q0, tile_rows)
            qs[rows, :] = (q_ref[here, cols].astype(F32) * scale).astype(BF)
            grad = da_ref[here, cols]
            das[rows, :] = grad
            both = grad.astype(F32) * att_ref[here, cols].astype(F32)
            deltas.append(jnp.sum(both.T, axis=0, keepdims=True))
        delta = jnp.concatenate(deltas, axis=1)
        bits_row = bits_ref[tile]
        lse_row = lse_ref[tile]
        q_pos = query_places(tile, tile_rows, heads)
        free, count = tile_plan(tile, per_tile)

        def step(masked, j, acc):
            k0 = chunk_start(tile, j, per_tile)
            at = pl.ds(k0, CHUNK)
            keys = k_ref[at, :]
            p = jnp.exp(dot_nt(keys, qs[...]) - lse_row)
            if masked:
                p = jnp.where(seen(k0, bits_row, q_pos, seg_len), p, 0.0)
            dp = dot_nt(v_ref[at, :], das[...])
            ds = (p * (dp - delta)).astype(BF)
            dv[at, :] += dot32(p.astype(BF), das[...])
            dk[at, :] += dot32(ds, qs[...])
            return acc + dot_tn(keys, ds)

        acc = lax.fori_loop(0, free, functools.partial(step, False), jnp.zeros((HD, width), F32))
        acc = lax.fori_loop(free, count, functools.partial(step, True), acc)
        out = (acc * scale).T
        at = pl.ds(q0, tile_rows)
        for h in range(heads):
            grad = out[h * tile_rows : (h + 1) * tile_rows, :]
            dq_ref[at, h * HD : (h + 1) * HD] = rotate(grad, cos_ref[at, :], -sin_ref[at, :]).astype(BF)
        return carry

    lax.fori_loop(0, 5, one_tile, 0)
    dk_ref[...] = dk[...].astype(BF)
    dv_ref[...] = dv[...].astype(BF)


def attention(bits, q, k, v, heads, seg_len):
    tree_len = q.shape[0]
    width = heads * 4 * seg_len
    work = heads * tree_len * tree_len // 2
    return pl.pallas_call(
        functools.partial(attn_fwd_kernel, heads, seg_len),
        out_shape=(
            jax.ShapeDtypeStruct((tree_len, heads * HD), BF),
            jax.ShapeDtypeStruct((5, 1, width), F32),
        ),
        in_specs=[pl.BlockSpec(memory_space=pltpu.VMEM)] * 4,
        out_specs=(pl.BlockSpec(memory_space=pltpu.VMEM),) * 2,
        scratch_shapes=[pltpu.VMEM((width, HD), BF), pltpu.VMEM((16 * seg_len, width), F32)],
        compiler_params=pltpu.CompilerParams(vmem_limit_bytes=VMEM_LIMIT),
        cost_estimate=pl.CostEstimate(flops=4 * HD * work, bytes_accessed=6 * tree_len * HD * 2, transcendentals=work),
        name="attn_fwd",
    )(bits, q, k, v)


def attention_back(bits, lse, cosines, sines, q, k, v, attended, da, heads, seg_len):
    tree_len = q.shape[0]
    width = heads * 4 * seg_len
    work = heads * tree_len * tree_len // 2
    return pl.pallas_call(
        functools.partial(attn_bwd_kernel, heads, seg_len),
        out_shape=(
            jax.ShapeDtypeStruct((tree_len, heads * HD), BF),
            jax.ShapeDtypeStruct((tree_len, HD), BF),
            jax.ShapeDtypeStruct((tree_len, HD), BF),
        ),
        in_specs=[pl.BlockSpec(memory_space=pltpu.VMEM)] * 9,
        out_specs=(pl.BlockSpec(memory_space=pltpu.VMEM),) * 3,
        scratch_shapes=[
            pltpu.VMEM((width, HD), BF),
            pltpu.VMEM((width, HD), BF),
            pltpu.VMEM((tree_len, HD), F32),
            pltpu.VMEM((tree_len, HD), F32),
        ],
        compiler_params=pltpu.CompilerParams(vmem_limit_bytes=VMEM_LIMIT),
        cost_estimate=pl.CostEstimate(flops=10 * HD * work, bytes_accessed=12 * tree_len * HD * 2, transcendentals=work),
        name="attn_bwd",
    )(bits, lse, cosines, sines, q, k, v, attended, da)


def whole(shape):
    return pl.BlockSpec(shape, lambda i: (0,) * len(shape), pipeline_mode=pl.Buffered(1))


def by_rows(rows, width):
    return pl.BlockSpec((rows, width), lambda i: (i, 0))


def project_kernel(heads, latent_width, x_ref, w_ref, qup_ref, g1_ref, gl_ref, cos_ref, sin_ref, q_ref, k_ref, v_ref, l_ref):
    x = x_ref[...].astype(F32)
    normed = (x * rms_scale(x) * g1_ref[...]).astype(BF)
    latent = dot32(normed, w_ref[:, :latent_width])
    latent_in = (latent * rms_scale(latent) * gl_ref[...]).astype(BF)
    l_ref[...] = latent_in
    cosines, sines = cos_ref[...], sin_ref[...]
    both = dot32(normed, w_ref[:, latent_width : latent_width + 2 * HD])
    k_ref[...] = rotate(both[:, :HD], cosines, sines).astype(BF)
    v_ref[...] = both[:, HD:].astype(BF)
    query = dot32(latent_in, qup_ref[...])
    for h in range(heads):
        at = slice(h * HD, (h + 1) * HD)
        q_ref[:, at] = rotate(query[:, at], cosines, sines).astype(BF)


def project(x, w_in, qup_cols, gain_one, gain_latent, cosines, sines, heads, rows):
    tree_len, model = x.shape
    latent_width = qup_cols.shape[0]
    outs = [(heads * HD, BF), (HD, BF), (HD, BF), (latent_width, BF)]
    flops = 2 * tree_len * (model * (latent_width + 2 * HD) + latent_width * heads * HD)
    return pl.pallas_call(
        functools.partial(project_kernel, heads, latent_width),
        grid=(tree_len // rows,),
        out_shape=[jax.ShapeDtypeStruct((tree_len, w), t) for w, t in outs],
        in_specs=[
            by_rows(rows, model),
            whole(w_in.shape),
            whole(qup_cols.shape),
            whole((1, model)),
            whole((1, latent_width)),
            by_rows(rows, HD // 2),
            by_rows(rows, HD // 2),
        ],
        out_specs=[by_rows(rows, w) for w, _ in outs],
        compiler_params=pltpu.CompilerParams(vmem_limit_bytes=VMEM_LIMIT),
        cost_estimate=pl.CostEstimate(flops=flops, bytes_accessed=tree_len * 10000 + w_in.size * 2, transcendentals=0),
        name="project",
    )(x, w_in, qup_cols, gain_one[None], gain_latent[None], cosines, sines)


def ffn_kernel(mid_ref, cot_ref, wg_ref, wu_ref, wd_ref, act_ref, gg_ref, ug_ref, part_ref):
    mid = mid_ref[...]
    gate = dot32(mid, wg_ref[...])
    up = dot32(mid, wu_ref[...])
    grad = dot_nt(cot_ref[...], wd_ref[...])
    sig = jax.nn.sigmoid(gate)
    silu = gate * sig
    act_ref[...] = (silu * up).astype(BF)
    gate_grad = (grad * up * sig * (1.0 + gate * (1.0 - sig))).astype(BF)
    up_grad = (grad * silu).astype(BF)
    gg_ref[...] = gate_grad
    ug_ref[...] = up_grad
    part_ref[...] = (dot_nt(gate_grad, wg_ref[...]) + dot_nt(up_grad, wu_ref[...])).astype(BF)


def ffn(mid, cot, gate_cols, up_cols, down_rows, rows):
    count, model = mid.shape
    units = gate_cols.shape[1]
    outs = [(units, BF)] * 3 + [(model, BF)]
    return pl.pallas_call(
        ffn_kernel,
        grid=(count // rows,),
        out_shape=[jax.ShapeDtypeStruct((count, w), t) for w, t in outs],
        in_specs=[by_rows(rows, model)] * 2 + [whole(gate_cols.shape)] * 2 + [whole(down_rows.shape)],
        out_specs=[by_rows(rows, w) for w, _ in outs],
        compiler_params=pltpu.CompilerParams(vmem_limit_bytes=VMEM_LIMIT),
        cost_estimate=pl.CostEstimate(
            flops=10 * count * model * units, bytes_accessed=6 * (count + units) * model, transcendentals=count * units
        ),
        name="ffn",
    )(mid, cot, gate_cols, up_cols, down_rows)


def unit_grad_kernel(mid_ref, grad_ref, out_ref, turned):
    @pl.when(pl.program_id(0) == 0)
    def _():
        turned[...] = grad_ref[...].T

    out_ref[0] = dot32(turned[...], mid_ref[...]).astype(BF)


def unit_grads(mid, grad, parts):
    count, model = mid.shape
    units = grad.shape[1]
    wide = model // parts
    return pl.pallas_call(
        unit_grad_kernel,
        grid=(parts,),
        out_shape=jax.ShapeDtypeStruct((parts, units, wide), BF),
        in_specs=[pl.BlockSpec((count, wide), lambda i: (0, i)), whole(grad.shape)],
        out_specs=pl.BlockSpec((1, units, wide), lambda i: (i, 0, 0)),
        scratch_shapes=[pltpu.VMEM((units, count), BF)],
        compiler_params=pltpu.CompilerParams(vmem_limit_bytes=VMEM_LIMIT),
        cost_estimate=pl.CostEstimate(
            flops=2 * count * model * units, bytes_accessed=2 * (count + units) * model, transcendentals=0
        ),
        name="unit_grads",
    )(mid, grad)


def body(
    hidden_in,
    segment_ids,
    parents,
    norm_gain,
    w_qdown,
    q_gain,
    w_qup,
    w_key,
    w_value,
    w_out,
    ffn_gain,
    w_gate,
    w_up,
    w_down,
    cotangent,
):
    rows, model = hidden_in.shape
    dn, cn = lax.axis_size("dp"), lax.axis_size("c")
    zn, sn = lax.axis_size(LINE), lax.axis_size(SHARE)
    fn = lax.axis_size(TREE)
    heads = H // fn
    latent_width = w_qdown.shape[1]
    in_width = latent_width + 2 * HD
    per_row, per_latent = norm_gain.shape[0], q_gain.shape[0]
    d_at, c_at, f_at = lax.axis_index("dp"), lax.axis_index("c"), lax.axis_index(TREE)
    tree_len = rows * fn
    seg_len = tree_len // NSEG
    block_rows = 2 * rows

    def exchange(parts, axes):
        return lax.all_to_all(parts, axes, split_axis=0, concat_axis=0, tiled=True)

    def spread(block, axes):
        return exchange(jnp.broadcast_to(block[None], (lax.axis_size(axes),) + block.shape), axes)

    def total(parts, axes):
        return jnp.sum(exchange(parts.astype(BF), axes).astype(F32), axis=0)

    def other_core(a):
        return lax.ppermute(a, "c", [(c, (c + 1) % cn) for c in range(cn)])

    def by_core(mine, axis):
        came = other_core(mine)
        return jnp.stack([jnp.where(c_at == 0, mine, came), jnp.where(c_at == 0, came, mine)], axis=axis)

    def exchange_share(parts):
        if sn != cn:
            return exchange(parts, SHARE)
        came = other_core(at_index(parts, 1 - c_at))
        return jnp.stack([jnp.where(c_at == 0, parts[0], came), jnp.where(c_at == 0, came, parts[1])])

    def at_index(a, index, axis=0):
        return lax.dynamic_index_in_dim(a, index, axis, keepdims=False)

    def plain(a):
        return with_layout_constraint(a, Layout(major_to_minor=tuple(range(a.ndim))))

    def after(a, *before):
        return lax.optimization_barrier((a,) + before)[0]

    def own_rows(a):
        return lax.dynamic_slice_in_dim(a, f_at * rows, rows, 0)

    def tree_gather(block):
        return lax.all_gather(block, TREE, axis=0, tiled=True)

    def tree_scatter(parts):
        return lax.psum_scatter(parts, TREE, scatter_dimension=0, tiled=True).astype(F32)

    def over_dp(a, m):
        return lax.ppermute(a, "dp", [(d, d ^ m) for d in range(dn)])

    def spread_dp(block):
        out = jnp.zeros((dn,) + block.shape, block.dtype)
        for m in range(dn):
            got = over_dp(block, m) if m else block
            out = lax.dynamic_update_index_in_dim(out, got, d_at ^ m, 0)
        return out

    def spread_line(block):
        out = jnp.zeros((zn,) + block.shape, block.dtype)
        z_at = lax.axis_index(LINE)
        for m in range(zn):
            got = lax.ppermute(block, LINE, [(z, (z + m) % zn) for z in range(zn)]) if m else block
            out = lax.dynamic_update_index_in_dim(out, got, (z_at + zn - m) % zn, 0)
        return out

    tags = -(-rows // per_row)
    extra = jnp.concatenate(
        [
            norm_gain[:, None],
            ffn_gain[:, None],
            jnp.pad(q_gain, (0, per_row - per_latent))[:, None],
            jnp.pad(segment_ids.astype(BF), (0, tags * per_row - rows)).reshape(tags, per_row).T,
            jnp.zeros((per_row, 125 - tags), BF),
        ],
        axis=1,
    )
    x_all = tree_gather(hidden_in)
    in_block = jnp.concatenate([w_qdown, w_key, w_value, extra], axis=1)
    qup_rows, out_rows, unit_rows = w_qup.shape[0], w_out.shape[0], w_down.shape[0]
    qn, units = fn // sn, dn * unit_rows

    def unit_columns(weight):
        return jnp.transpose(weight.reshape(per_row, dn, fn, unit_rows), (2, 0, 1, 3)).reshape(fn, per_row, units)

    unit_sent = jnp.stack([unit_columns(w_gate), unit_columns(w_up)], axis=1)
    qup_cols = jnp.transpose(w_qup.reshape(qup_rows, sn, heads, qn, HD), (3, 1, 0, 2, 4))
    qup_cols = exchange(qup_cols.reshape(fn, qup_rows, heads * HD), TREE)
    out_cols = spread_dp(w_out).reshape(sn, heads, out_rows, model)
    in_line = after(spread_line(in_block), qup_cols, unit_sent)
    qup_cols = spread_dp(qup_cols).reshape(latent_width, heads * HD)
    out_cols = jnp.swapaxes(exchange_share(out_cols), 0, 1).reshape(heads * HD, model)
    in_full = by_core(after(spread(in_line, "dp"), qup_cols, out_cols), 2).reshape(model, in_width + 128)
    w_in = in_full[:, :in_width]
    extra = in_full[:, in_width:].T.astype(F32)
    gain_one, gain_two = extra[0], extra[1]
    gain_latent = extra[2].reshape(dn * fn, per_row)[:, :per_latent].reshape(latent_width)
    run_labels = lax.dynamic_slice_in_dim(extra[3 : 3 + tags].reshape(tags, dn, fn, per_row), d_at, 1, 1)[:, 0]
    run_labels = jnp.swapaxes(run_labels, 0, 1).reshape(fn, tags * per_row)[:, :rows]
    run_labels = run_labels.reshape(tree_len)[::seg_len].astype(jnp.int32)

    cot = tree_gather(after(cotangent, x_all))

    labels = jnp.arange(NSEG, dtype=jnp.int32)
    reach = jnp.maximum(
        (labels[:, None] == labels[None, :]).astype(F32), (parents[0][:, None] == labels[None, :]).astype(F32)
    )
    for _ in range(5):
        reach = jnp.minimum(jnp.dot(reach, reach, precision=HIGHEST), 1.0)
    pick_run = (run_labels[:, None] == labels[None, :]).astype(F32)
    run_reach = jnp.dot(jnp.dot(pick_run, reach, precision=HIGHEST), pick_run.T, precision=HIGHEST)
    run_depth = jnp.sum(run_reach, axis=1) - 1.0
    run_bits = jnp.sum(jnp.where(run_reach > 0.5, jnp.left_shift(1, labels)[None, :], 0), axis=1).astype(jnp.int32)
    bits = jnp.broadcast_to(run_bits.reshape(5, 1, 4, 1), (5, heads, 4, seg_len)).reshape(5, 1, heads * 4 * seg_len)
    inverse = ROPE_BASE ** (-(jnp.arange(HD // 2, dtype=F32) * 2.0) / HD)
    coarse = (run_depth * seg_len)[:, None] * inverse[None, :]
    fine = jnp.arange(seg_len, dtype=F32)[:, None] * inverse[None, :]
    cos_a, sin_a = jnp.cos(coarse)[:, None, :], jnp.sin(coarse)[:, None, :]
    cos_b, sin_b = jnp.cos(fine)[None, :, :], jnp.sin(fine)[None, :, :]
    cosines = (cos_a * cos_b - sin_a * sin_b).reshape(tree_len, HD // 2)
    sines = (sin_a * cos_b + cos_a * sin_b).reshape(tree_len, HD // 2)

    query_all, key_all, value_all, latent_in = project(
        x_all, in_full, qup_cols, gain_one, gain_latent, cosines, sines, heads, block_rows
    )
    unit_cols = exchange(after(unit_sent, x_all), TREE)
    attended, lse = attention(bits, query_all, key_all, value_all, heads, seg_len)
    x = hidden_in.astype(F32)
    out_part = dot32(after(attended, cot, unit_cols), out_cols).astype(BF)
    gate_cols = spread(unit_cols[:, 0], "dp").reshape(model, units)
    up_cols = spread(after(unit_cols[:, 1], gate_cols), "dp").reshape(model, units)
    scale_one = rms_scale(x)
    normed_one = x * scale_one
    normed_in = (normed_one * gain_one).astype(BF)
    latent = dot32(after(normed_in, out_part), w_in[:, :latent_width])
    scale_latent = rms_scale(latent)

    def per_core(a, core):
        return at_index(a.reshape(a.shape[0], dn * zn, cn, per_row), core, 2).reshape(a.shape[0], dn * zn * per_row)

    normed_kept, normed_sent = per_core(normed_in, c_at), per_core(normed_in, 1 - c_at)
    mixed = x + after(tree_scatter(out_part), gate_cols, scale_latent, normed_kept, normed_sent)
    mixed = lax.optimization_barrier(mixed)
    down_rows = spread_dp(after(w_down, out_part)).reshape(units, model)

    scale_two = rms_scale(mixed)
    normed_two = mixed * scale_two
    normed_mid = (normed_two * gain_two).astype(BF)
    mid = after(tree_gather(normed_mid), down_rows, gate_cols, up_cols)
    activated, gate_grad, up_grad, mid_part = ffn(mid, cot, gate_cols, up_cols, down_rows, block_rows)
    gate_parts = unit_grads(after(mid, mid_part), gate_grad, dn)
    down_parts = dot_tn(after(activated, gate_parts), cot).astype(BF).reshape(dn, unit_rows, model)
    up_parts = unit_grads(after(mid, down_parts), up_grad, dn)
    gate_parts = exchange(gate_parts, "dp")
    down_parts = exchange(after(down_parts, gate_parts), "dp")
    mid_grad = after(tree_scatter(mid_part), down_parts, up_parts)
    up_parts = exchange(after(up_parts, down_parts), "dp")
    layer_part = dot32(after(activated, up_grad), down_rows).astype(BF)
    mixed_back = norm_back(mid_grad, normed_two, scale_two, gain_two)
    gain_two_cols = gain_column(mid_grad, normed_two, 1)
    mixed_grad = lax.optimization_barrier(cotangent.astype(F32) + mixed_back)
    branch_grad = mixed_grad.astype(BF)

    grad_down = jnp.sum(down_parts.astype(F32), axis=0)

    def unit_sum(parts):
        return jnp.sum(parts.astype(F32), axis=0).astype(BF).reshape(units, fn, per_row)

    unit_own = jnp.stack([unit_sum(gate_parts), unit_sum(up_parts)])
    unit_own = plain(jnp.transpose(unit_own, (2, 0, 3, 1)))
    branch, layer_part, gain_two_cols, unit_own, grad_down = lax.optimization_barrier(
        (tree_gather(branch_grad), layer_part, gain_two_cols, unit_own, grad_down)
    )
    unit_own = exchange(unit_own, TREE).reshape(fn, 2, per_row, dn, unit_rows)
    attended_grad = dot_nt(branch, out_cols).astype(BF)
    query_grad, key_part, value_part = attention_back(
        bits, lse, cosines, sines, query_all, key_all, value_all, attended, attended_grad, heads, seg_len
    )
    latent_part = dot_nt(query_grad, qup_cols).astype(BF)
    back_part = after(jnp.concatenate([latent_part, key_part, value_part], axis=1), unit_own)
    out_grads = jnp.swapaxes(
        dot_tn(attended, after(branch, back_part)).astype(BF).reshape(heads, sn, out_rows, model), 0, 1
    )
    out_grads = exchange_share(out_grads).reshape(dn, out_rows, model)
    grad_out = at_index(out_grads, d_at).astype(F32)
    for m in range(1, dn):
        grad_out = grad_out + over_dp(at_index(out_grads, d_at ^ m), m).astype(F32)
    grad_qup = dot_tn(latent_in, after(query_grad, back_part, out_grads))
    grad_qup = total(grad_qup.reshape(dn, fn * qup_rows, heads * HD), "dp").astype(BF)
    grad_qup = exchange(grad_qup.reshape(fn, qup_rows, heads * HD), TREE).reshape(qn, sn, qup_rows, heads, HD)
    unit_own = jnp.transpose(unit_own, (1, 2, 3, 0, 4)).reshape(2, per_row, dn * fn * unit_rows).astype(F32)
    back, grad_qup, grad_out, grad_gate, grad_up = lax.optimization_barrier(
        (tree_scatter(back_part), grad_qup, grad_out, plain(unit_own[0]), plain(unit_own[1]))
    )
    layer_out = (mixed + tree_scatter(after(layer_part, back))).astype(BF)
    grad_qup = jnp.transpose(grad_qup, (2, 1, 3, 0, 4)).reshape(qup_rows, H * HD).astype(F32)

    normed_latent = latent * scale_latent
    latent_back = norm_back(back[:, :latent_width], normed_latent, scale_latent, gain_latent)
    key_grad = rotate(back[:, latent_width : latent_width + HD], own_rows(cosines), -own_rows(sines))
    in_grad = jnp.concatenate([latent_back, key_grad, back[:, latent_width + HD :]], axis=1).astype(BF)

    in_own = other_core(dot_tn(normed_sent, in_grad).astype(BF)).astype(F32) + dot_tn(normed_kept, in_grad)
    in_own = in_own.astype(BF).reshape(dn, zn, per_row, in_width)
    in_parts = exchange(in_own, "dp")
    in_late, back_late, _ = lax.optimization_barrier((in_grad, back, in_own))
    normed_grad = dot_nt(in_late, w_in)
    input_back = norm_back(normed_grad, normed_one, scale_one, gain_one)
    grad_in = (mixed_grad + input_back).astype(BF)
    in_sum = total(jnp.sum(in_parts.astype(F32), axis=0), LINE)

    gain_cols = gain_column(back_late[:, :latent_width], normed_latent, 2).reshape(dn * fn, per_latent, 128)
    gain_cols = jnp.pad(gain_cols, ((0, 0), (0, per_row - per_latent), (0, 0))).reshape(model, 128)
    gain_cols = gain_cols + gain_two_cols + gain_column(normed_grad, normed_one, 0)
    gain_cols = gain_cols.reshape(dn, zn, cn, per_row, 128)
    gain_own = other_core(at_index(gain_cols, 1 - c_at, 2).astype(BF)).astype(F32) + at_index(gain_cols, c_at, 2)
    gain_own = after(gain_own, in_parts)
    gain_sum = at_index(gain_own, d_at)
    for m in range(1, dn):
        gain_sum = gain_sum + over_dp(at_index(gain_own, d_at ^ m).astype(BF), m).astype(F32)
    gain_line, z_at = gain_sum, lax.axis_index(LINE)
    gain_sum = at_index(gain_line, z_at)
    for m in range(1, zn):
        sent = at_index(gain_line, (z_at + m) % zn).astype(BF)
        gain_sum = gain_sum + lax.ppermute(sent, LINE, [(z, (z + m) % zn) for z in range(zn)]).astype(F32)
    return (
        layer_out,
        grad_in,
        gain_sum[:, 0],
        in_sum[:, :latent_width],
        gain_sum[:per_latent, 2],
        grad_qup,
        in_sum[:, latent_width : latent_width + HD],
        in_sum[:, latent_width + HD : in_width],
        grad_out,
        gain_sum[:, 1],
        grad_gate,
        grad_up,
        grad_down,
    )


def solution(mesh):
    dn, fn = mesh.shape["dp"], mesh.shape["fsdp"]
    share = dn * fn // H
    fine = jax.sharding.Mesh(mesh.devices.reshape(dn, fn // share, share // 2, 2), ("dp",) + TREE)
    split = P(("dp",) + TREE, None)
    line = P(("dp",) + TREE)
    placed = (
        split, line, P("dp", None), line, split, line, split, split, split, split, line, split, split, split, split,
    )
    given = (split, split, line, split, line, split, split, split, split, line, split, split, split)
    return jax.shard_map(body, mesh=fine, in_specs=placed, out_specs=given, check_vma=False)
```

```python
import functools

import jax
import jax.numpy as jnp
from jax import lax
from jax.experimental import pallas as pl
from jax.experimental.layout import Layout, with_layout_constraint
from jax.experimental.pallas import tpu as pltpu
from jax.sharding import PartitionSpec as P

H = 16
HD = 256
NSEG = 20

EPSILON = 1e-06
ROPE_BASE = 10000.0
HIGHEST = lax.Precision.HIGHEST
NEGATIVE = -1e30
BF = jnp.bfloat16
F32 = jnp.float32
CHUNK = 320
TREE = ("q", "r", "c")
LINE = ("q", "r")
SHARE = ("r", "c")
VMEM_LIMIT = 56 * 1024 * 1024


def dot32(a, b):
    return jnp.dot(a, b, preferred_element_type=F32)


def dot_nt(a, b):
    return lax.dot_general(a, b, (((1,), (1,)), ((), ())), preferred_element_type=F32)


def dot_tn(a, b):
    return lax.dot_general(a, b, (((0,), (0,)), ((), ())), preferred_element_type=F32)


def rms_scale(values):
    return lax.rsqrt(jnp.mean(values * values, axis=-1, keepdims=True) + EPSILON)


def norm_back(upstream, normed, row_scale, gain_vec):
    scaled = upstream * gain_vec
    inner_mean = jnp.mean(scaled * normed, axis=-1, keepdims=True)
    return row_scale * (scaled - normed * inner_mean)


def gain_column(upstream, normed, column):
    picked = (lax.broadcasted_iota(jnp.int32, (upstream.shape[0], 128), 1) == column).astype(F32)
    return lax.dot_general(
        upstream * normed, picked, (((0,), (0,)), ((), ())), precision=HIGHEST, preferred_element_type=F32
    )


def rotate(values, cosines, sines):
    half = values.shape[-1] // 2
    a, b = values[..., :half], values[..., half:]
    return jnp.concatenate([a * cosines - b * sines, b * cosines + a * sines], axis=-1)


def tile_plan(tile, per_tile):
    free = jnp.minimum(tile, 2) * per_tile
    count = jnp.where(tile == 4, 4, tile + 1) * per_tile
    return free, count


def chunk_start(tile, j, per_tile):
    jump = jnp.where((tile == 4) & (j >= 3 * per_tile), per_tile, 0)
    return pl.multiple_of((j + jump) * CHUNK, CHUNK)


def seen(k0, bits_row, q_pos, seg_len):
    shape = (CHUNK, q_pos.shape[1])
    key_pos = lax.broadcasted_iota(jnp.int32, (CHUNK, 1), 0) + k0
    key_bit = jnp.left_shift(jnp.int32(1), key_pos // seg_len)
    reach = jnp.broadcast_to(key_bit, shape) & jnp.broadcast_to(bits_row, shape)
    return (reach != 0) & (jnp.broadcast_to(key_pos, shape) <= jnp.broadcast_to(q_pos, shape))


def query_places(tile, tile_rows, heads):
    lane = lax.broadcasted_iota(jnp.int32, (1, heads * tile_rows), 1)
    return tile * tile_rows + lax.rem(lane, tile_rows)


def attn_fwd_kernel(heads, seg_len, bits_ref, q_ref, k_ref, v_ref, wo_ref, att_ref, lse_ref, part_ref, qs, st):
    tile_rows = 4 * seg_len
    width = heads * tile_rows
    per_tile = tile_rows // CHUNK
    scale = HD ** (-0.5)

    def one_tile(tile, carry):
        q0 = pl.multiple_of(tile * tile_rows, tile_rows)
        for h in range(heads):
            rows = q_ref[pl.ds(q0, tile_rows), h * HD : (h + 1) * HD]
            qs[h * tile_rows : (h + 1) * tile_rows, :] = (rows.astype(F32) * scale).astype(BF)
        bits_row = bits_ref[tile]
        q_pos = query_places(tile, tile_rows, heads)
        free, count = tile_plan(tile, per_tile)

        def score(masked, j, top):
            k0 = chunk_start(tile, j, per_tile)
            s = dot_nt(k_ref[pl.ds(k0, CHUNK), :], qs[...])
            if masked:
                s = jnp.where(seen(k0, bits_row, q_pos, seg_len), s, NEGATIVE)
            st[pl.ds(pl.multiple_of(j * CHUNK, CHUNK), CHUNK), :] = s
            return jnp.maximum(top, jnp.max(s, axis=0, keepdims=True))

        top = lax.fori_loop(0, free, functools.partial(score, False), jnp.full((1, width), NEGATIVE, F32))
        top = lax.fori_loop(free, count, functools.partial(score, True), top)

        def gather(j, carry):
            total, acc = carry
            k0 = chunk_start(tile, j, per_tile)
            p = jnp.exp(st[pl.ds(pl.multiple_of(j * CHUNK, CHUNK), CHUNK), :] - top)
            acc = acc + dot_tn(v_ref[pl.ds(k0, CHUNK), :], p.astype(BF))
            return total + jnp.sum(p, axis=0, keepdims=True), acc

        total, out = lax.fori_loop(0, count, gather, (jnp.zeros((1, width), F32), jnp.zeros((HD, width), F32)))
        lse_ref[tile] = top + jnp.log(total)
        out = (out * (1.0 / total)).T.astype(BF)
        here = pl.ds(q0, tile_rows)
        part = None
        for h in range(heads):
            cols = slice(h * HD, (h + 1) * HD)
            own = out[h * tile_rows : (h + 1) * tile_rows, :]
            att_ref[here, cols] = own
            more = dot32(own, wo_ref[cols, :])
            part = more if part is None else part + more
        part_ref[here, :] = part.astype(BF)
        return carry

    lax.fori_loop(0, 5, one_tile, 0)


def attn_bwd_kernel(
    heads, seg_len, bits_ref, lse_ref, cos_ref, sin_ref, q_ref, k_ref, v_ref, att_ref, branch_ref, wo_ref, wq_ref,
    dq_ref, back_ref, qs, das, dk, dv,
):
    tile_rows = 4 * seg_len
    width = heads * tile_rows
    per_tile = tile_rows // CHUNK
    scale = HD ** (-0.5)
    dk[...] = jnp.zeros_like(dk)
    dv[...] = jnp.zeros_like(dv)

    def one_tile(tile, carry):
        q0 = pl.multiple_of(tile * tile_rows, tile_rows)
        deltas = []
        for h in range(heads):
            rows = slice(h * tile_rows, (h + 1) * tile_rows)
            cols = slice(h * HD, (h + 1) * HD)
            here = pl.ds(q0, tile_rows)
            qs[rows, :] = (q_ref[here, cols].astype(F32) * scale).astype(BF)
            grad = dot_nt(branch_ref[here, :], wo_ref[cols, :]).astype(BF)
            das[rows, :] = grad
            both = grad.astype(F32) * att_ref[here, cols].astype(F32)
            deltas.append(jnp.sum(both.T, axis=0, keepdims=True))
        delta = jnp.concatenate(deltas, axis=1)
        bits_row = bits_ref[tile]
        lse_row = lse_ref[tile]
        q_pos = query_places(tile, tile_rows, heads)
        free, count = tile_plan(tile, per_tile)

        def step(masked, j, acc):
            k0 = chunk_start(tile, j, per_tile)
            at = pl.ds(k0, CHUNK)
            keys = k_ref[at, :]
            p = jnp.exp(dot_nt(keys, qs[...]) - lse_row)
            if masked:
                p = jnp.where(seen(k0, bits_row, q_pos, seg_len), p, 0.0)
            dp = dot_nt(v_ref[at, :], das[...])
            ds = (p * (dp - delta)).astype(BF)
            dv[at, :] += dot32(p.astype(BF), das[...])
            dk[at, :] += dot32(ds, qs[...])
            return acc + dot_tn(keys, ds)

        acc = lax.fori_loop(0, free, functools.partial(step, False), jnp.zeros((HD, width), F32))
        acc = lax.fori_loop(free, count, functools.partial(step, True), acc)
        out = (acc * scale).T
        at = pl.ds(q0, tile_rows)
        latent = None
        for h in range(heads):
            cols = slice(h * HD, (h + 1) * HD)
            grad = out[h * tile_rows : (h + 1) * tile_rows, :]
            grad = rotate(grad, cos_ref[at, :], -sin_ref[at, :]).astype(BF)
            dq_ref[at, cols] = grad
            more = dot_nt(grad, wq_ref[:, cols])
            latent = more if latent is None else latent + more
        back_ref[at, :latent_width] = latent.astype(BF)
        return carry

    latent_width = wq_ref.shape[0]
    lax.fori_loop(0, 5, one_tile, 0)
    back_ref[:, latent_width : latent_width + HD] = dk[...].astype(BF)
    back_ref[:, latent_width + HD :] = dv[...].astype(BF)


def attention(bits, q, k, v, out_cols, heads, seg_len):
    tree_len = q.shape[0]
    width = heads * 4 * seg_len
    work = heads * tree_len * tree_len // 2
    return pl.pallas_call(
        functools.partial(attn_fwd_kernel, heads, seg_len),
        out_shape=(
            jax.ShapeDtypeStruct((tree_len, heads * HD), BF),
            jax.ShapeDtypeStruct((5, 1, width), F32),
            jax.ShapeDtypeStruct((tree_len, out_cols.shape[1]), BF),
        ),
        in_specs=[pl.BlockSpec(memory_space=pltpu.VMEM)] * 5,
        out_specs=(pl.BlockSpec(memory_space=pltpu.VMEM),) * 3,
        scratch_shapes=[pltpu.VMEM((width, HD), BF), pltpu.VMEM((16 * seg_len, width), F32)],
        compiler_params=pltpu.CompilerParams(vmem_limit_bytes=VMEM_LIMIT),
        cost_estimate=pl.CostEstimate(flops=6 * HD * work, bytes_accessed=6 * tree_len * HD * 2, transcendentals=work),
        name="attn_fwd",
    )(bits, q, k, v, out_cols)


def attention_back(bits, lse, cosines, sines, q, k, v, attended, branch, out_cols, qup_cols, heads, seg_len):
    tree_len = q.shape[0]
    width = heads * 4 * seg_len
    work = heads * tree_len * tree_len // 2
    return pl.pallas_call(
        functools.partial(attn_bwd_kernel, heads, seg_len),
        out_shape=(
            jax.ShapeDtypeStruct((tree_len, heads * HD), BF),
            jax.ShapeDtypeStruct((tree_len, qup_cols.shape[0] + 2 * HD), BF),
        ),
        in_specs=[pl.BlockSpec(memory_space=pltpu.VMEM)] * 11,
        out_specs=(pl.BlockSpec(memory_space=pltpu.VMEM),) * 2,
        scratch_shapes=[
            pltpu.VMEM((width, HD), BF),
            pltpu.VMEM((width, HD), BF),
            pltpu.VMEM((tree_len, HD), F32),
            pltpu.VMEM((tree_len, HD), F32),
        ],
        compiler_params=pltpu.CompilerParams(vmem_limit_bytes=VMEM_LIMIT),
        cost_estimate=pl.CostEstimate(flops=14 * HD * work, bytes_accessed=12 * tree_len * HD * 2, transcendentals=work),
        name="attn_bwd",
    )(bits, lse, cosines, sines, q, k, v, attended, branch, out_cols, qup_cols)


def whole(shape):
    return pl.BlockSpec(shape, lambda i: (0,) * len(shape), pipeline_mode=pl.Buffered(1))


def by_rows(rows, width):
    return pl.BlockSpec((rows, width), lambda i: (i, 0))


def project_kernel(heads, latent_width, x_ref, w_ref, qup_ref, g1_ref, gl_ref, cos_ref, sin_ref, q_ref, k_ref, v_ref, l_ref):
    x = x_ref[...].astype(F32)
    normed = (x * rms_scale(x) * g1_ref[...]).astype(BF)
    latent = dot32(normed, w_ref[:, :latent_width])
    latent_in = (latent * rms_scale(latent) * gl_ref[...]).astype(BF)
    l_ref[...] = latent_in
    cosines, sines = cos_ref[...], sin_ref[...]
    both = dot32(normed, w_ref[:, latent_width : latent_width + 2 * HD])
    k_ref[...] = rotate(both[:, :HD], cosines, sines).astype(BF)
    v_ref[...] = both[:, HD:].astype(BF)
    query = dot32(latent_in, qup_ref[...])
    for h in range(heads):
        at = slice(h * HD, (h + 1) * HD)
        q_ref[:, at] = rotate(query[:, at], cosines, sines).astype(BF)


def project(x, w_in, qup_cols, gain_one, gain_latent, cosines, sines, heads, rows):
    tree_len, model = x.shape
    latent_width = qup_cols.shape[0]
    outs = [(heads * HD, BF), (HD, BF), (HD, BF), (latent_width, BF)]
    flops = 2 * tree_len * (model * (latent_width + 2 * HD) + latent_width * heads * HD)
    return pl.pallas_call(
        functools.partial(project_kernel, heads, latent_width),
        grid=(tree_len // rows,),
        out_shape=[jax.ShapeDtypeStruct((tree_len, w), t) for w, t in outs],
        in_specs=[
            by_rows(rows, model),
            whole(w_in.shape),
            whole(qup_cols.shape),
            whole((1, model)),
            whole((1, latent_width)),
            by_rows(rows, HD // 2),
            by_rows(rows, HD // 2),
        ],
        out_specs=[by_rows(rows, w) for w, _ in outs],
        compiler_params=pltpu.CompilerParams(vmem_limit_bytes=VMEM_LIMIT),
        cost_estimate=pl.CostEstimate(flops=flops, bytes_accessed=tree_len * 10000 + w_in.size * 2, transcendentals=0),
        name="project",
    )(x, w_in, qup_cols, gain_one[None], gain_latent[None], cosines, sines)


def ffn_kernel(mid_ref, cot_ref, wg_ref, wu_ref, wd_ref, act_ref, gg_ref, ug_ref, part_ref):
    mid = mid_ref[...]
    gate = dot32(mid, wg_ref[...])
    up = dot32(mid, wu_ref[...])
    grad = dot_nt(cot_ref[...], wd_ref[...])
    sig = jax.nn.sigmoid(gate)
    silu = gate * sig
    act_ref[...] = (silu * up).astype(BF)
    gate_grad = (grad * up * sig * (1.0 + gate * (1.0 - sig))).astype(BF)
    up_grad = (grad * silu).astype(BF)
    gg_ref[...] = gate_grad
    ug_ref[...] = up_grad
    part_ref[...] = (dot_nt(gate_grad, wg_ref[...]) + dot_nt(up_grad, wu_ref[...])).astype(BF)


def ffn(mid, cot, gate_cols, up_cols, down_rows, rows):
    count, model = mid.shape
    units = gate_cols.shape[1]
    outs = [(units, BF)] * 3 + [(model, BF)]
    return pl.pallas_call(
        ffn_kernel,
        grid=(count // rows,),
        out_shape=[jax.ShapeDtypeStruct((count, w), t) for w, t in outs],
        in_specs=[by_rows(rows, model)] * 2 + [whole(gate_cols.shape)] * 2 + [whole(down_rows.shape)],
        out_specs=[by_rows(rows, w) for w, _ in outs],
        compiler_params=pltpu.CompilerParams(vmem_limit_bytes=VMEM_LIMIT),
        cost_estimate=pl.CostEstimate(
            flops=10 * count * model * units, bytes_accessed=6 * (count + units) * model, transcendentals=count * units
        ),
        name="ffn",
    )(mid, cot, gate_cols, up_cols, down_rows)


def unit_grad_kernel(mid_ref, grad_ref, out_ref, turned):
    @pl.when(pl.program_id(0) == 0)
    def _():
        turned[...] = grad_ref[...].T

    out_ref[0] = dot32(turned[...], mid_ref[...]).astype(BF)


def unit_grads(mid, grad, parts):
    count, model = mid.shape
    units = grad.shape[1]
    wide = model // parts
    return pl.pallas_call(
        unit_grad_kernel,
        grid=(parts,),
        out_shape=jax.ShapeDtypeStruct((parts, units, wide), BF),
        in_specs=[pl.BlockSpec((count, wide), lambda i: (0, i)), whole(grad.shape)],
        out_specs=pl.BlockSpec((1, units, wide), lambda i: (i, 0, 0)),
        scratch_shapes=[pltpu.VMEM((units, count), BF)],
        compiler_params=pltpu.CompilerParams(vmem_limit_bytes=VMEM_LIMIT),
        cost_estimate=pl.CostEstimate(
            flops=2 * count * model * units, bytes_accessed=2 * (count + units) * model, transcendentals=0
        ),
        name="unit_grads",
    )(mid, grad)


def body(
    hidden_in,
    segment_ids,
    parents,
    norm_gain,
    w_qdown,
    q_gain,
    w_qup,
    w_key,
    w_value,
    w_out,
    ffn_gain,
    w_gate,
    w_up,
    w_down,
    cotangent,
):
    rows, model = hidden_in.shape
    dn, cn = lax.axis_size("dp"), lax.axis_size("c")
    zn, sn = lax.axis_size(LINE), lax.axis_size(SHARE)
    fn = lax.axis_size(TREE)
    heads = H // fn
    latent_width = w_qdown.shape[1]
    in_width = latent_width + 2 * HD
    per_row, per_latent = norm_gain.shape[0], q_gain.shape[0]
    d_at, c_at, f_at = lax.axis_index("dp"), lax.axis_index("c"), lax.axis_index(TREE)
    tree_len = rows * fn
    seg_len = tree_len // NSEG
    block_rows = 2 * rows

    def exchange(parts, axes):
        return lax.all_to_all(parts, axes, split_axis=0, concat_axis=0, tiled=True)

    def spread(block, axes):
        return exchange(jnp.broadcast_to(block[None], (lax.axis_size(axes),) + block.shape), axes)

    def total(parts, axes):
        return jnp.sum(exchange(parts.astype(BF), axes).astype(F32), axis=0)

    def other_core(a):
        return lax.ppermute(a, "c", [(c, (c + 1) % cn) for c in range(cn)])

    def by_core(mine, axis):
        came = other_core(mine)
        return jnp.stack([jnp.where(c_at == 0, mine, came), jnp.where(c_at == 0, came, mine)], axis=axis)

    def exchange_share(parts):
        if sn != cn:
            return exchange(parts, SHARE)
        came = other_core(at_index(parts, 1 - c_at))
        return jnp.stack([jnp.where(c_at == 0, parts[0], came), jnp.where(c_at == 0, came, parts[1])])

    def at_index(a, index, axis=0):
        return lax.dynamic_index_in_dim(a, index, axis, keepdims=False)

    def plain(a):
        return with_layout_constraint(a, Layout(major_to_minor=tuple(range(a.ndim))))

    def after(a, *before):
        return lax.optimization_barrier((a,) + before)[0]

    def own_rows(a):
        return lax.dynamic_slice_in_dim(a, f_at * rows, rows, 0)

    def tree_gather(block):
        return lax.all_gather(block, TREE, axis=0, tiled=True)

    def tree_scatter(parts):
        return lax.psum_scatter(parts, TREE, scatter_dimension=0, tiled=True).astype(F32)

    def over_dp(a, m):
        return lax.ppermute(a, "dp", [(d, d ^ m) for d in range(dn)])

    def spread_dp(block):
        out = jnp.zeros((dn,) + block.shape, block.dtype)
        for m in range(dn):
            got = over_dp(block, m) if m else block
            out = lax.dynamic_update_index_in_dim(out, got, d_at ^ m, 0)
        return out

    def spread_line(block):
        out = jnp.zeros((zn,) + block.shape, block.dtype)
        z_at = lax.axis_index(LINE)
        for m in range(zn):
            got = lax.ppermute(block, LINE, [(z, (z + m) % zn) for z in range(zn)]) if m else block
            out = lax.dynamic_update_index_in_dim(out, got, (z_at + zn - m) % zn, 0)
        return out

    tags = -(-rows // per_row)
    extra = jnp.concatenate(
        [
            norm_gain[:, None],
            ffn_gain[:, None],
            jnp.pad(q_gain, (0, per_row - per_latent))[:, None],
            jnp.pad(segment_ids.astype(BF), (0, tags * per_row - rows)).reshape(tags, per_row).T,
            jnp.zeros((per_row, 125 - tags), BF),
        ],
        axis=1,
    )
    x_all = tree_gather(hidden_in)
    in_block = jnp.concatenate([w_qdown, w_key, w_value, extra], axis=1)
    qup_rows, out_rows, unit_rows = w_qup.shape[0], w_out.shape[0], w_down.shape[0]
    qn, units = fn // sn, dn * unit_rows

    def unit_columns(weight):
        return jnp.transpose(weight.reshape(per_row, dn, fn, unit_rows), (2, 0, 1, 3)).reshape(fn, per_row, units)

    unit_sent = jnp.stack([unit_columns(w_gate), unit_columns(w_up)], axis=1)
    qup_cols = jnp.transpose(w_qup.reshape(qup_rows, sn, heads, qn, HD), (3, 1, 0, 2, 4))
    qup_cols = exchange(qup_cols.reshape(fn, qup_rows, heads * HD), TREE)
    out_cols = spread_dp(w_out).reshape(sn, heads, out_rows, model)
    in_line = after(spread_line(in_block), qup_cols, unit_sent, out_cols)
    in_wide = spread(in_line, "dp")
    qup_cols = spread(after(qup_cols, in_wide), "dp").reshape(latent_width, heads * HD)
    in_full = by_core(in_wide, 2).reshape(model, in_width + 128)
    w_in = in_full[:, :in_width]
    extra = in_full[:, in_width:].T.astype(F32)
    gain_one, gain_two = extra[0], extra[1]
    gain_latent = extra[2].reshape(dn * fn, per_row)[:, :per_latent].reshape(latent_width)
    run_labels = lax.dynamic_slice_in_dim(extra[3 : 3 + tags].reshape(tags, dn, fn, per_row), d_at, 1, 1)[:, 0]
    run_labels = jnp.swapaxes(run_labels, 0, 1).reshape(fn, tags * per_row)[:, :rows]
    run_labels = run_labels.reshape(tree_len)[::seg_len].astype(jnp.int32)

    cot = tree_gather(after(cotangent, x_all))

    labels = jnp.arange(NSEG, dtype=jnp.int32)
    reach = jnp.maximum(
        (labels[:, None] == labels[None, :]).astype(F32), (parents[0][:, None] == labels[None, :]).astype(F32)
    )
    for _ in range(5):
        reach = jnp.minimum(jnp.dot(reach, reach, precision=HIGHEST), 1.0)
    pick_run = (run_labels[:, None] == labels[None, :]).astype(F32)
    run_reach = jnp.dot(jnp.dot(pick_run, reach, precision=HIGHEST), pick_run.T, precision=HIGHEST)
    run_depth = jnp.sum(run_reach, axis=1) - 1.0
    run_bits = jnp.sum(jnp.where(run_reach > 0.5, jnp.left_shift(1, labels)[None, :], 0), axis=1).astype(jnp.int32)
    bits = jnp.broadcast_to(run_bits.reshape(5, 1, 4, 1), (5, heads, 4, seg_len)).reshape(5, 1, heads * 4 * seg_len)
    inverse = ROPE_BASE ** (-(jnp.arange(HD // 2, dtype=F32) * 2.0) / HD)
    coarse = (run_depth * seg_len)[:, None] * inverse[None, :]
    fine = jnp.arange(seg_len, dtype=F32)[:, None] * inverse[None, :]
    cos_a, sin_a = jnp.cos(coarse)[:, None, :], jnp.sin(coarse)[:, None, :]
    cos_b, sin_b = jnp.cos(fine)[None, :, :], jnp.sin(fine)[None, :, :]
    cosines = (cos_a * cos_b - sin_a * sin_b).reshape(tree_len, HD // 2)
    sines = (sin_a * cos_b + cos_a * sin_b).reshape(tree_len, HD // 2)

    query_all, key_all, value_all, latent_in = project(
        x_all, in_full, qup_cols, gain_one, gain_latent, cosines, sines, heads, block_rows
    )
    unit_cols = exchange(after(unit_sent, x_all, qup_cols), TREE)
    out_cols = jnp.swapaxes(exchange_share(after(out_cols, key_all)), 0, 1).reshape(heads * HD, model)
    attended, lse, out_part = attention(bits, query_all, key_all, value_all, out_cols, heads, seg_len)
    x = hidden_in.astype(F32)
    out_part = after(out_part, cot, unit_cols)
    gate_cols = spread(unit_cols[:, 0], "dp").reshape(model, units)
    up_cols = spread(after(unit_cols[:, 1], out_part), "dp").reshape(model, units)
    scale_one = rms_scale(x)
    normed_one = x * scale_one
    normed_in = (normed_one * gain_one).astype(BF)
    latent = dot32(after(normed_in, out_part), w_in[:, :latent_width])
    scale_latent = rms_scale(latent)

    def per_core(a, core):
        return at_index(a.reshape(a.shape[0], dn * zn, cn, per_row), core, 2).reshape(a.shape[0], dn * zn * per_row)

    normed_kept, normed_sent = per_core(normed_in, c_at), per_core(normed_in, 1 - c_at)
    down_rows = spread(after(w_down, gate_cols), "dp").reshape(units, model)
    mixed = x + after(tree_scatter(out_part), gate_cols, down_rows, scale_latent, normed_kept, normed_sent)
    mixed = lax.optimization_barrier(mixed)

    scale_two = rms_scale(mixed)
    normed_two = mixed * scale_two
    normed_mid = (normed_two * gain_two).astype(BF)
    mid = after(tree_gather(normed_mid), down_rows, gate_cols, up_cols)
    activated, gate_grad, up_grad, mid_part = ffn(mid, cot, gate_cols, up_cols, down_rows, block_rows)
    gate_parts = unit_grads(after(mid, mid_part), gate_grad, dn)
    down_parts = dot_tn(after(activated, gate_parts), cot).astype(BF).reshape(dn, unit_rows, model)
    up_parts = unit_grads(after(mid, down_parts), up_grad, dn)
    gate_parts = exchange(gate_parts, "dp")
    mid_grad = after(tree_scatter(mid_part), gate_parts, down_parts, up_parts)
    up_parts = exchange(after(up_parts, gate_parts), "dp")
    down_parts = exchange(after(down_parts, up_parts), "dp")
    layer_part = dot32(after(activated, up_grad), down_rows).astype(BF)
    mixed_back = norm_back(mid_grad, normed_two, scale_two, gain_two)
    gain_two_cols = gain_column(mid_grad, normed_two, 1)
    mixed_grad = lax.optimization_barrier(cotangent.astype(F32) + mixed_back)
    branch_grad = mixed_grad.astype(BF)

    grad_down = jnp.sum(down_parts.astype(F32), axis=0)

    def unit_sum(parts):
        return jnp.sum(parts.astype(F32), axis=0).astype(BF).reshape(units, fn, per_row)

    unit_own = jnp.stack([unit_sum(gate_parts), unit_sum(up_parts)])
    unit_own = plain(jnp.transpose(unit_own, (2, 0, 3, 1)))
    branch, layer_part, gain_two_cols, unit_own, grad_down = lax.optimization_barrier(
        (tree_gather(branch_grad), layer_part, gain_two_cols, unit_own, grad_down)
    )
    unit_own = exchange(unit_own, TREE).reshape(fn, 2, per_row, dn, unit_rows)
    query_grad, back_part = attention_back(
        bits, lse, cosines, sines, query_all, key_all, value_all, attended, branch, out_cols, qup_cols, heads, seg_len
    )
    back_part = after(back_part, unit_own)
    out_grads = jnp.swapaxes(
        dot_tn(attended, after(branch, back_part)).astype(BF).reshape(heads, sn, out_rows, model), 0, 1
    )
    out_grads = exchange_share(out_grads).reshape(dn, out_rows, model)
    grad_out = at_index(out_grads, d_at).astype(F32)
    for m in range(1, dn):
        grad_out = grad_out + over_dp(at_index(out_grads, d_at ^ m), m).astype(F32)
    grad_qup = dot_tn(latent_in, after(query_grad, back_part, out_grads))
    grad_qup = total(grad_qup.reshape(dn, fn * qup_rows, heads * HD), "dp").astype(BF)
    grad_qup = exchange(grad_qup.reshape(fn, qup_rows, heads * HD), TREE).reshape(qn, sn, qup_rows, heads, HD)
    unit_own = jnp.transpose(unit_own, (1, 2, 3, 0, 4)).reshape(2, per_row, dn * fn * unit_rows).astype(F32)
    back, grad_qup, grad_out, grad_gate, grad_up = lax.optimization_barrier(
        (tree_scatter(back_part), grad_qup, grad_out, plain(unit_own[0]), plain(unit_own[1]))
    )
    layer_out = (mixed + tree_scatter(after(layer_part, back))).astype(BF)
    grad_qup = jnp.transpose(grad_qup, (2, 1, 3, 0, 4)).reshape(qup_rows, H * HD).astype(F32)

    normed_latent = latent * scale_latent
    latent_back = norm_back(back[:, :latent_width], normed_latent, scale_latent, gain_latent)
    key_grad = rotate(back[:, latent_width : latent_width + HD], own_rows(cosines), -own_rows(sines))
    in_grad = jnp.concatenate([latent_back, key_grad, back[:, latent_width + HD :]], axis=1).astype(BF)

    in_own = other_core(dot_tn(normed_sent, in_grad).astype(BF)).astype(F32) + dot_tn(normed_kept, in_grad)
    in_own = in_own.astype(BF).reshape(dn, zn, per_row, in_width)
    in_parts = exchange(in_own, "dp")
    in_late, back_late, _ = lax.optimization_barrier((in_grad, back, in_own))
    normed_grad = dot_nt(in_late, w_in)
    input_back = norm_back(normed_grad, normed_one, scale_one, gain_one)
    grad_in = (mixed_grad + input_back).astype(BF)
    in_line_parts = jnp.sum(in_parts.astype(F32), axis=0).astype(BF)
    in_sum = total(in_line_parts, LINE)

    gain_cols = gain_column(back_late[:, :latent_width], normed_latent, 2).reshape(dn * fn, per_latent, 128)
    gain_cols = jnp.pad(gain_cols, ((0, 0), (0, per_row - per_latent), (0, 0))).reshape(model, 128)
    gain_cols = gain_cols + gain_two_cols + gain_column(normed_grad, normed_one, 0)
    gain_cols = gain_cols.reshape(dn, zn, cn, per_row, 128)
    gain_own = other_core(at_index(gain_cols, 1 - c_at, 2).astype(BF)).astype(F32) + at_index(gain_cols, c_at, 2)
    gain_own = after(gain_own, in_line_parts)
    gain_sum = at_index(gain_own, d_at)
    for m in range(1, dn):
        gain_sum = gain_sum + over_dp(at_index(gain_own, d_at ^ m).astype(BF), m).astype(F32)
    gain_line, z_at = gain_sum, lax.axis_index(LINE)
    gain_sum = at_index(gain_line, z_at)
    for m in range(1, zn):
        sent = at_index(gain_line, (z_at + m) % zn).astype(BF)
        gain_sum = gain_sum + lax.ppermute(sent, LINE, [(z, (z + m) % zn) for z in range(zn)]).astype(F32)
    return (
        layer_out,
        grad_in,
        gain_sum[:, 0],
        in_sum[:, :latent_width],
        gain_sum[:per_latent, 2],
        grad_qup,
        in_sum[:, latent_width : latent_width + HD],
        in_sum[:, latent_width + HD : in_width],
        grad_out,
        gain_sum[:, 1],
        grad_gate,
        grad_up,
        grad_down,
    )


def solution(mesh):
    dn, fn = mesh.shape["dp"], mesh.shape["fsdp"]
    share = dn * fn // H
    fine = jax.sharding.Mesh(mesh.devices.reshape(dn, fn // share, share // 2, 2), ("dp",) + TREE)
    split = P(("dp",) + TREE, None)
    line = P(("dp",) + TREE)
    placed = (
        split, line, P("dp", None), line, split, line, split, split, split, split, line, split, split, split, split,
    )
    given = (split, split, line, split, line, split, split, split, split, line, split, split, split)
    return jax.shard_map(body, mesh=fine, in_specs=placed, out_specs=given, check_vma=False)
```

```python
import functools

import jax
import jax.numpy as jnp
from jax import lax
from jax.experimental import pallas as pl
from jax.experimental.layout import Layout, with_layout_constraint
from jax.experimental.pallas import tpu as pltpu
from jax.sharding import PartitionSpec as P

H = 16
HD = 256
NSEG = 20

EPSILON = 1e-06
ROPE_BASE = 10000.0
HIGHEST = lax.Precision.HIGHEST
NEGATIVE = -1e30
BF = jnp.bfloat16
F32 = jnp.float32
CHUNK = 320
TREE = ("q", "r", "c")
LINE = ("q", "r")
SHARE = ("r", "c")
VMEM_LIMIT = 56 * 1024 * 1024


def dot32(a, b):
    return jnp.dot(a, b, preferred_element_type=F32)


def dot_nt(a, b):
    return lax.dot_general(a, b, (((1,), (1,)), ((), ())), preferred_element_type=F32)


def dot_tn(a, b):
    return lax.dot_general(a, b, (((0,), (0,)), ((), ())), preferred_element_type=F32)


def rms_scale(values):
    return lax.rsqrt(jnp.mean(values * values, axis=-1, keepdims=True) + EPSILON)


def norm_back(upstream, normed, row_scale, gain_vec):
    scaled = upstream * gain_vec
    inner_mean = jnp.mean(scaled * normed, axis=-1, keepdims=True)
    return row_scale * (scaled - normed * inner_mean)


def gain_column(upstream, normed, column):
    picked = (lax.broadcasted_iota(jnp.int32, (upstream.shape[0], 128), 1) == column).astype(F32)
    return lax.dot_general(
        upstream * normed, picked, (((0,), (0,)), ((), ())), precision=HIGHEST, preferred_element_type=F32
    )


def rotate(values, cosines, sines):
    half = values.shape[-1] // 2
    a, b = values[..., :half], values[..., half:]
    return jnp.concatenate([a * cosines - b * sines, b * cosines + a * sines], axis=-1)


def tile_plan(tile, per_tile):
    free = jnp.minimum(tile, 2) * per_tile
    count = jnp.where(tile == 4, 4, tile + 1) * per_tile
    return free, count


def chunk_start(tile, j, per_tile):
    jump = jnp.where((tile == 4) & (j >= 3 * per_tile), per_tile, 0)
    return pl.multiple_of((j + jump) * CHUNK, CHUNK)


def seen(k0, bits_row, q_pos, seg_len):
    shape = (CHUNK, q_pos.shape[1])
    key_pos = lax.broadcasted_iota(jnp.int32, (CHUNK, 1), 0) + k0
    key_bit = jnp.left_shift(jnp.int32(1), key_pos // seg_len)
    reach = jnp.broadcast_to(key_bit, shape) & jnp.broadcast_to(bits_row, shape)
    return (reach != 0) & (jnp.broadcast_to(key_pos, shape) <= jnp.broadcast_to(q_pos, shape))


def query_places(tile, tile_rows, heads):
    lane = lax.broadcasted_iota(jnp.int32, (1, heads * tile_rows), 1)
    return tile * tile_rows + lax.rem(lane, tile_rows)


def attn_fwd_kernel(heads, seg_len, bits_ref, q_ref, k_ref, v_ref, wo_ref, att_ref, lse_ref, part_ref, qs, st):
    tile_rows = 4 * seg_len
    width = heads * tile_rows
    per_tile = tile_rows // CHUNK
    scale = HD ** (-0.5)

    def one_tile(tile, carry):
        q0 = pl.multiple_of(tile * tile_rows, tile_rows)
        for h in range(heads):
            rows = q_ref[pl.ds(q0, tile_rows), h * HD : (h + 1) * HD]
            qs[h * tile_rows : (h + 1) * tile_rows, :] = (rows.astype(F32) * scale).astype(BF)
        bits_row = bits_ref[tile]
        q_pos = query_places(tile, tile_rows, heads)
        free, count = tile_plan(tile, per_tile)

        def score(masked, j, top):
            k0 = chunk_start(tile, j, per_tile)
            s = dot_nt(k_ref[pl.ds(k0, CHUNK), :], qs[...])
            if masked:
                s = jnp.where(seen(k0, bits_row, q_pos, seg_len), s, NEGATIVE)
            st[pl.ds(pl.multiple_of(j * CHUNK, CHUNK), CHUNK), :] = s
            return jnp.maximum(top, jnp.max(s, axis=0, keepdims=True))

        top = lax.fori_loop(0, free, functools.partial(score, False), jnp.full((1, width), NEGATIVE, F32))
        top = lax.fori_loop(free, count, functools.partial(score, True), top)

        def gather(j, carry):
            total, acc = carry
            k0 = chunk_start(tile, j, per_tile)
            p = jnp.exp(st[pl.ds(pl.multiple_of(j * CHUNK, CHUNK), CHUNK), :] - top)
            acc = acc + dot_tn(v_ref[pl.ds(k0, CHUNK), :], p.astype(BF))
            return total + jnp.sum(p, axis=0, keepdims=True), acc

        total, out = lax.fori_loop(0, count, gather, (jnp.zeros((1, width), F32), jnp.zeros((HD, width), F32)))
        lse_ref[tile] = top + jnp.log(total)
        out = (out * (1.0 / total)).T.astype(BF)
        here = pl.ds(q0, tile_rows)
        part = None
        for h in range(heads):
            cols = slice(h * HD, (h + 1) * HD)
            own = out[h * tile_rows : (h + 1) * tile_rows, :]
            att_ref[here, cols] = own
            more = dot32(own, wo_ref[cols, :])
            part = more if part is None else part + more
        part_ref[here, :] = part.astype(BF)
        return carry

    lax.fori_loop(0, 5, one_tile, 0)


def attn_bwd_kernel(
    heads, seg_len, bits_ref, lse_ref, cos_ref, sin_ref, q_ref, k_ref, v_ref, att_ref, branch_ref, wo_ref, wq_ref,
    dq_ref, back_ref, qs, das, dk, dv,
):
    tile_rows = 4 * seg_len
    width = heads * tile_rows
    per_tile = tile_rows // CHUNK
    scale = HD ** (-0.5)
    dk[...] = jnp.zeros_like(dk)
    dv[...] = jnp.zeros_like(dv)

    def one_tile(tile, carry):
        q0 = pl.multiple_of(tile * tile_rows, tile_rows)
        deltas = []
        for h in range(heads):
            rows = slice(h * tile_rows, (h + 1) * tile_rows)
            cols = slice(h * HD, (h + 1) * HD)
            here = pl.ds(q0, tile_rows)
            qs[rows, :] = (q_ref[here, cols].astype(F32) * scale).astype(BF)
            grad = dot_nt(branch_ref[here, :], wo_ref[cols, :]).astype(BF)
            das[rows, :] = grad
            both = grad.astype(F32) * att_ref[here, cols].astype(F32)
            deltas.append(jnp.sum(both.T, axis=0, keepdims=True))
        delta = jnp.concatenate(deltas, axis=1)
        bits_row = bits_ref[tile]
        lse_row = lse_ref[tile]
        q_pos = query_places(tile, tile_rows, heads)
        free, count = tile_plan(tile, per_tile)

        def step(masked, j, acc):
            k0 = chunk_start(tile, j, per_tile)
            at = pl.ds(k0, CHUNK)
            keys = k_ref[at, :]
            p = jnp.exp(dot_nt(keys, qs[...]) - lse_row)
            if masked:
                p = jnp.where(seen(k0, bits_row, q_pos, seg_len), p, 0.0)
            dp = dot_nt(v_ref[at, :], das[...])
            ds = (p * (dp - delta)).astype(BF)
            dv[at, :] += dot32(p.astype(BF), das[...])
            dk[at, :] += dot32(ds, qs[...])
            return acc + dot_tn(keys, ds)

        acc = lax.fori_loop(0, free, functools.partial(step, False), jnp.zeros((HD, width), F32))
        acc = lax.fori_loop(free, count, functools.partial(step, True), acc)
        out = (acc * scale).T
        at = pl.ds(q0, tile_rows)
        latent = None
        for h in range(heads):
            cols = slice(h * HD, (h + 1) * HD)
            grad = out[h * tile_rows : (h + 1) * tile_rows, :]
            grad = rotate(grad, cos_ref[at, :], -sin_ref[at, :]).astype(BF)
            dq_ref[at, cols] = grad
            more = dot_nt(grad, wq_ref[:, cols])
            latent = more if latent is None else latent + more
        back_ref[at, :latent_width] = latent.astype(BF)
        return carry

    latent_width = wq_ref.shape[0]
    lax.fori_loop(0, 5, one_tile, 0)
    back_ref[:, latent_width : latent_width + HD] = dk[...].astype(BF)
    back_ref[:, latent_width + HD :] = dv[...].astype(BF)


def attention(bits, q, k, v, out_cols, heads, seg_len):
    tree_len = q.shape[0]
    width = heads * 4 * seg_len
    work = heads * tree_len * tree_len // 2
    return pl.pallas_call(
        functools.partial(attn_fwd_kernel, heads, seg_len),
        out_shape=(
            jax.ShapeDtypeStruct((tree_len, heads * HD), BF),
            jax.ShapeDtypeStruct((5, 1, width), F32),
            jax.ShapeDtypeStruct((tree_len, out_cols.shape[1]), BF),
        ),
        in_specs=[pl.BlockSpec(memory_space=pltpu.VMEM)] * 5,
        out_specs=(pl.BlockSpec(memory_space=pltpu.VMEM),) * 3,
        scratch_shapes=[pltpu.VMEM((width, HD), BF), pltpu.VMEM((16 * seg_len, width), F32)],
        compiler_params=pltpu.CompilerParams(vmem_limit_bytes=VMEM_LIMIT),
        cost_estimate=pl.CostEstimate(flops=6 * HD * work, bytes_accessed=6 * tree_len * HD * 2, transcendentals=work),
        name="attn_fwd",
    )(bits, q, k, v, out_cols)


def attention_back(bits, lse, cosines, sines, q, k, v, attended, branch, out_cols, qup_cols, heads, seg_len):
    tree_len = q.shape[0]
    width = heads * 4 * seg_len
    work = heads * tree_len * tree_len // 2
    return pl.pallas_call(
        functools.partial(attn_bwd_kernel, heads, seg_len),
        out_shape=(
            jax.ShapeDtypeStruct((tree_len, heads * HD), BF),
            jax.ShapeDtypeStruct((tree_len, qup_cols.shape[0] + 2 * HD), BF),
        ),
        in_specs=[pl.BlockSpec(memory_space=pltpu.VMEM)] * 11,
        out_specs=(pl.BlockSpec(memory_space=pltpu.VMEM),) * 2,
        scratch_shapes=[
            pltpu.VMEM((width, HD), BF),
            pltpu.VMEM((width, HD), BF),
            pltpu.VMEM((tree_len, HD), F32),
            pltpu.VMEM((tree_len, HD), F32),
        ],
        compiler_params=pltpu.CompilerParams(vmem_limit_bytes=VMEM_LIMIT),
        cost_estimate=pl.CostEstimate(flops=14 * HD * work, bytes_accessed=12 * tree_len * HD * 2, transcendentals=work),
        name="attn_bwd",
    )(bits, lse, cosines, sines, q, k, v, attended, branch, out_cols, qup_cols)


def whole(shape):
    return pl.BlockSpec(shape, lambda i: (0,) * len(shape), pipeline_mode=pl.Buffered(1))


def by_rows(rows, width):
    return pl.BlockSpec((rows, width), lambda i: (i, 0))


def project_kernel(heads, latent_width, x_ref, w_ref, qup_ref, g1_ref, gl_ref, cos_ref, sin_ref, q_ref, k_ref, v_ref, l_ref):
    x = x_ref[...].astype(F32)
    normed = (x * rms_scale(x) * g1_ref[...]).astype(BF)
    latent = dot32(normed, w_ref[:, :latent_width])
    latent_in = (latent * rms_scale(latent) * gl_ref[...]).astype(BF)
    l_ref[...] = latent_in
    cosines, sines = cos_ref[...], sin_ref[...]
    both = dot32(normed, w_ref[:, latent_width : latent_width + 2 * HD])
    k_ref[...] = rotate(both[:, :HD], cosines, sines).astype(BF)
    v_ref[...] = both[:, HD:].astype(BF)
    query = dot32(latent_in, qup_ref[...])
    for h in range(heads):
        at = slice(h * HD, (h + 1) * HD)
        q_ref[:, at] = rotate(query[:, at], cosines, sines).astype(BF)


def project(x, w_in, qup_cols, gain_one, gain_latent, cosines, sines, heads, rows):
    tree_len, model = x.shape
    latent_width = qup_cols.shape[0]
    outs = [(heads * HD, BF), (HD, BF), (HD, BF), (latent_width, BF)]
    flops = 2 * tree_len * (model * (latent_width + 2 * HD) + latent_width * heads * HD)
    return pl.pallas_call(
        functools.partial(project_kernel, heads, latent_width),
        grid=(tree_len // rows,),
        out_shape=[jax.ShapeDtypeStruct((tree_len, w), t) for w, t in outs],
        in_specs=[
            by_rows(rows, model),
            whole(w_in.shape),
            whole(qup_cols.shape),
            whole((1, model)),
            whole((1, latent_width)),
            by_rows(rows, HD // 2),
            by_rows(rows, HD // 2),
        ],
        out_specs=[by_rows(rows, w) for w, _ in outs],
        compiler_params=pltpu.CompilerParams(vmem_limit_bytes=VMEM_LIMIT),
        cost_estimate=pl.CostEstimate(flops=flops, bytes_accessed=tree_len * 10000 + w_in.size * 2, transcendentals=0),
        name="project",
    )(x, w_in, qup_cols, gain_one[None], gain_latent[None], cosines, sines)


def ffn_kernel(mid_ref, cot_ref, wg_ref, wu_ref, wd_ref, act_ref, gg_ref, ug_ref, part_ref):
    mid = mid_ref[...]
    gate = dot32(mid, wg_ref[...])
    up = dot32(mid, wu_ref[...])
    grad = dot_nt(cot_ref[...], wd_ref[...])
    sig = jax.nn.sigmoid(gate)
    silu = gate * sig
    act_ref[...] = (silu * up).astype(BF)
    gate_grad = (grad * up * sig * (1.0 + gate * (1.0 - sig))).astype(BF)
    up_grad = (grad * silu).astype(BF)
    gg_ref[...] = gate_grad
    ug_ref[...] = up_grad
    part_ref[...] = (dot_nt(gate_grad, wg_ref[...]) + dot_nt(up_grad, wu_ref[...])).astype(BF)


def ffn(mid, cot, gate_cols, up_cols, down_rows, rows):
    count, model = mid.shape
    units = gate_cols.shape[1]
    outs = [(units, BF)] * 3 + [(model, BF)]
    return pl.pallas_call(
        ffn_kernel,
        grid=(count // rows,),
        out_shape=[jax.ShapeDtypeStruct((count, w), t) for w, t in outs],
        in_specs=[by_rows(rows, model)] * 2 + [whole(gate_cols.shape)] * 2 + [whole(down_rows.shape)],
        out_specs=[by_rows(rows, w) for w, _ in outs],
        compiler_params=pltpu.CompilerParams(vmem_limit_bytes=VMEM_LIMIT),
        cost_estimate=pl.CostEstimate(
            flops=10 * count * model * units, bytes_accessed=6 * (count + units) * model, transcendentals=count * units
        ),
        name="ffn",
    )(mid, cot, gate_cols, up_cols, down_rows)


def unit_grad_kernel(mid_ref, grad_ref, out_ref, turned):
    @pl.when(pl.program_id(0) == 0)
    def _():
        turned[...] = grad_ref[...].T

    out_ref[0] = dot32(turned[...], mid_ref[...]).astype(BF)


def unit_grads(mid, grad, parts):
    count, model = mid.shape
    units = grad.shape[1]
    wide = model // parts
    return pl.pallas_call(
        unit_grad_kernel,
        grid=(parts,),
        out_shape=jax.ShapeDtypeStruct((parts, units, wide), BF),
        in_specs=[pl.BlockSpec((count, wide), lambda i: (0, i)), whole(grad.shape)],
        out_specs=pl.BlockSpec((1, units, wide), lambda i: (i, 0, 0)),
        scratch_shapes=[pltpu.VMEM((units, count), BF)],
        compiler_params=pltpu.CompilerParams(vmem_limit_bytes=VMEM_LIMIT),
        cost_estimate=pl.CostEstimate(
            flops=2 * count * model * units, bytes_accessed=2 * (count + units) * model, transcendentals=0
        ),
        name="unit_grads",
    )(mid, grad)


def body(
    hidden_in,
    segment_ids,
    parents,
    norm_gain,
    w_qdown,
    q_gain,
    w_qup,
    w_key,
    w_value,
    w_out,
    ffn_gain,
    w_gate,
    w_up,
    w_down,
    cotangent,
):
    rows, model = hidden_in.shape
    dn, cn = lax.axis_size("dp"), lax.axis_size("c")
    zn, sn = lax.axis_size(LINE), lax.axis_size(SHARE)
    fn = lax.axis_size(TREE)
    heads = H // fn
    latent_width = w_qdown.shape[1]
    in_width = latent_width + 2 * HD
    per_row, per_latent = norm_gain.shape[0], q_gain.shape[0]
    d_at, c_at, f_at = lax.axis_index("dp"), lax.axis_index("c"), lax.axis_index(TREE)
    tree_len = rows * fn
    seg_len = tree_len // NSEG
    block_rows = 2 * rows

    def exchange(parts, axes):
        return lax.all_to_all(parts, axes, split_axis=0, concat_axis=0, tiled=True)

    def spread(block, axes):
        return exchange(jnp.broadcast_to(block[None], (lax.axis_size(axes),) + block.shape), axes)

    def total(parts, axes):
        return jnp.sum(exchange(parts.astype(BF), axes).astype(F32), axis=0)

    def other_core(a):
        return lax.ppermute(a, "c", [(c, (c + 1) % cn) for c in range(cn)])

    def by_core(mine, axis):
        came = other_core(mine)
        return jnp.stack([jnp.where(c_at == 0, mine, came), jnp.where(c_at == 0, came, mine)], axis=axis)

    def exchange_share(parts):
        if sn != cn:
            return exchange(parts, SHARE)
        came = other_core(at_index(parts, 1 - c_at))
        return jnp.stack([jnp.where(c_at == 0, parts[0], came), jnp.where(c_at == 0, came, parts[1])])

    def at_index(a, index, axis=0):
        return lax.dynamic_index_in_dim(a, index, axis, keepdims=False)

    def plain(a):
        return with_layout_constraint(a, Layout(major_to_minor=tuple(range(a.ndim))))

    def after(a, *before):
        return lax.optimization_barrier((a,) + before)[0]

    def own_rows(a):
        return lax.dynamic_slice_in_dim(a, f_at * rows, rows, 0)

    def tree_gather(block):
        return lax.all_gather(block, TREE, axis=0, tiled=True)

    def tree_scatter(parts):
        return lax.psum_scatter(parts, TREE, scatter_dimension=0, tiled=True).astype(F32)

    def over_dp(a, m):
        return lax.ppermute(a, "dp", [(d, d ^ m) for d in range(dn)])

    def spread_dp(block):
        out = jnp.zeros((dn,) + block.shape, block.dtype)
        for m in range(dn):
            got = over_dp(block, m) if m else block
            out = lax.dynamic_update_index_in_dim(out, got, d_at ^ m, 0)
        return out

    def spread_line(block):
        out = jnp.zeros((zn,) + block.shape, block.dtype)
        z_at = lax.axis_index(LINE)
        for m in range(zn):
            got = lax.ppermute(block, LINE, [(z, (z + m) % zn) for z in range(zn)]) if m else block
            out = lax.dynamic_update_index_in_dim(out, got, (z_at + zn - m) % zn, 0)
        return out

    tags = -(-rows // per_row)
    extra = jnp.concatenate(
        [
            norm_gain[:, None],
            ffn_gain[:, None],
            jnp.pad(q_gain, (0, per_row - per_latent))[:, None],
            jnp.pad(segment_ids.astype(BF), (0, tags * per_row - rows)).reshape(tags, per_row).T,
            jnp.zeros((per_row, 125 - tags), BF),
        ],
        axis=1,
    )
    x_all = tree_gather(hidden_in)
    in_block = jnp.concatenate([w_qdown, w_key, w_value, extra], axis=1)
    qup_rows, out_rows, unit_rows = w_qup.shape[0], w_out.shape[0], w_down.shape[0]
    qn, units = fn // sn, dn * unit_rows

    def unit_columns(weight):
        return jnp.transpose(weight.reshape(per_row, dn, fn, unit_rows), (2, 0, 1, 3)).reshape(fn, per_row, units)

    unit_sent = jnp.stack([unit_columns(w_gate), unit_columns(w_up)], axis=1)
    qup_cols = jnp.transpose(w_qup.reshape(qup_rows, sn, heads, qn, HD), (3, 1, 0, 2, 4))
    qup_cols = exchange(qup_cols.reshape(fn, qup_rows, heads * HD), TREE)
    out_cols = spread_dp(w_out).reshape(sn, heads, out_rows, model)
    in_line = after(spread_line(in_block), qup_cols, unit_sent, out_cols)
    in_wide = spread(in_line, "dp")
    qup_cols = spread(after(qup_cols, in_wide), "dp").reshape(latent_width, heads * HD)
    in_full = by_core(in_wide, 2).reshape(model, in_width + 128)
    w_in = in_full[:, :in_width]
    extra = in_full[:, in_width:].T.astype(F32)
    gain_one, gain_two = extra[0], extra[1]
    gain_latent = extra[2].reshape(dn * fn, per_row)[:, :per_latent].reshape(latent_width)
    run_labels = lax.dynamic_slice_in_dim(extra[3 : 3 + tags].reshape(tags, dn, fn, per_row), d_at, 1, 1)[:, 0]
    run_labels = jnp.swapaxes(run_labels, 0, 1).reshape(fn, tags * per_row)[:, :rows]
    run_labels = run_labels.reshape(tree_len)[::seg_len].astype(jnp.int32)

    cot = tree_gather(after(cotangent, x_all))

    labels = jnp.arange(NSEG, dtype=jnp.int32)
    reach = jnp.maximum(
        (labels[:, None] == labels[None, :]).astype(F32), (parents[0][:, None] == labels[None, :]).astype(F32)
    )
    for _ in range(5):
        reach = jnp.minimum(jnp.dot(reach, reach, precision=HIGHEST), 1.0)
    pick_run = (run_labels[:, None] == labels[None, :]).astype(F32)
    run_reach = jnp.dot(jnp.dot(pick_run, reach, precision=HIGHEST), pick_run.T, precision=HIGHEST)
    run_depth = jnp.sum(run_reach, axis=1) - 1.0
    run_bits = jnp.sum(jnp.where(run_reach > 0.5, jnp.left_shift(1, labels)[None, :], 0), axis=1).astype(jnp.int32)
    bits = jnp.broadcast_to(run_bits.reshape(5, 1, 4, 1), (5, heads, 4, seg_len)).reshape(5, 1, heads * 4 * seg_len)
    inverse = ROPE_BASE ** (-(jnp.arange(HD // 2, dtype=F32) * 2.0) / HD)
    coarse = (run_depth * seg_len)[:, None] * inverse[None, :]
    fine = jnp.arange(seg_len, dtype=F32)[:, None] * inverse[None, :]
    cos_a, sin_a = jnp.cos(coarse)[:, None, :], jnp.sin(coarse)[:, None, :]
    cos_b, sin_b = jnp.cos(fine)[None, :, :], jnp.sin(fine)[None, :, :]
    cosines = (cos_a * cos_b - sin_a * sin_b).reshape(tree_len, HD // 2)
    sines = (sin_a * cos_b + cos_a * sin_b).reshape(tree_len, HD // 2)

    query_all, key_all, value_all, latent_in = project(
        x_all, in_full, qup_cols, gain_one, gain_latent, cosines, sines, heads, block_rows
    )
    unit_cols = exchange(after(unit_sent, x_all, qup_cols), TREE)
    out_cols = jnp.swapaxes(exchange_share(after(out_cols, key_all)), 0, 1).reshape(heads * HD, model)
    attended, lse, out_part = attention(bits, query_all, key_all, value_all, out_cols, heads, seg_len)
    x = hidden_in.astype(F32)
    down_sent = after(w_down, x_all)
    down_got = [over_dp(down_sent, m) for m in range(1, dn)]
    out_part, _, _, *down_got = lax.optimization_barrier((out_part, cot, unit_cols, *down_got))
    gate_cols = spread(unit_cols[:, 0], "dp").reshape(model, units)
    up_cols = spread(after(unit_cols[:, 1], out_part), "dp").reshape(model, units)
    scale_one = rms_scale(x)
    normed_one = x * scale_one
    normed_in = (normed_one * gain_one).astype(BF)
    latent = dot32(after(normed_in, out_part), w_in[:, :latent_width])
    scale_latent = rms_scale(latent)

    def per_core(a, core):
        return at_index(a.reshape(a.shape[0], dn * zn, cn, per_row), core, 2).reshape(a.shape[0], dn * zn * per_row)

    normed_kept, normed_sent = per_core(normed_in, c_at), per_core(normed_in, 1 - c_at)
    down_rows = jnp.zeros((dn, unit_rows, model), BF)
    for m, got in enumerate([after(w_down, out_part)] + down_got):
        down_rows = lax.dynamic_update_index_in_dim(down_rows, got, d_at ^ m, 0)
    down_rows = down_rows.reshape(units, model)
    mixed = x + after(tree_scatter(out_part), gate_cols, down_rows, scale_latent, normed_kept, normed_sent)
    mixed = lax.optimization_barrier(mixed)

    scale_two = rms_scale(mixed)
    normed_two = mixed * scale_two
    normed_mid = (normed_two * gain_two).astype(BF)
    mid = after(tree_gather(normed_mid), down_rows, gate_cols, up_cols)
    activated, gate_grad, up_grad, mid_part = ffn(mid, cot, gate_cols, up_cols, down_rows, block_rows)
    gate_parts = unit_grads(after(mid, mid_part), gate_grad, dn)
    down_parts = dot_tn(after(activated, gate_parts), cot).astype(BF).reshape(dn, unit_rows, model)
    up_parts = unit_grads(after(mid, down_parts), up_grad, dn)
    gate_parts = exchange(gate_parts, "dp")
    mid_grad = after(tree_scatter(mid_part), gate_parts, down_parts, up_parts)
    up_parts = exchange(after(up_parts, gate_parts), "dp")
    layer_part = dot32(after(activated, up_grad), down_rows).astype(BF)
    mixed_back = norm_back(mid_grad, normed_two, scale_two, gain_two)
    gain_two_cols = gain_column(mid_grad, normed_two, 1)
    mixed_grad = lax.optimization_barrier(cotangent.astype(F32) + mixed_back)
    branch_grad = mixed_grad.astype(BF)


    def unit_sum(parts):
        return jnp.sum(parts.astype(F32), axis=0).astype(BF).reshape(units, fn, per_row)

    unit_own = jnp.stack([unit_sum(gate_parts), unit_sum(up_parts)])
    unit_own = plain(jnp.transpose(unit_own, (2, 0, 3, 1)))
    branch, layer_part, gain_two_cols, unit_own = lax.optimization_barrier(
        (tree_gather(branch_grad), layer_part, gain_two_cols, unit_own)
    )
    down_sent = after(down_parts, branch)
    down_got = [over_dp(at_index(down_sent, d_at ^ m), m) for m in range(1, dn)]
    unit_got = exchange(unit_own, TREE)
    query_grad, back_part = attention_back(
        bits, lse, cosines, sines, query_all, key_all, value_all, attended, branch, out_cols, qup_cols, heads, seg_len
    )
    back_part, unit_got, *down_got = lax.optimization_barrier((back_part, unit_got, *down_got))
    grad_down = at_index(down_sent, d_at).astype(F32)
    for got in down_got:
        grad_down = grad_down + got.astype(F32)
    out_grads = jnp.swapaxes(
        dot_tn(attended, after(branch, back_part)).astype(BF).reshape(heads, sn, out_rows, model), 0, 1
    )
    out_grads = exchange_share(out_grads).reshape(dn, out_rows, model)
    grad_out = at_index(out_grads, d_at).astype(F32)
    for m in range(1, dn):
        grad_out = grad_out + over_dp(at_index(out_grads, d_at ^ m), m).astype(F32)
    grad_qup = dot_tn(latent_in, after(query_grad, back_part, out_grads))
    grad_qup = total(grad_qup.reshape(dn, fn * qup_rows, heads * HD), "dp").astype(BF)
    grad_qup = exchange(grad_qup.reshape(fn, qup_rows, heads * HD), TREE).reshape(qn, sn, qup_rows, heads, HD)
    unit_own = after(unit_got, out_grads).reshape(fn, 2, per_row, dn, unit_rows)
    unit_own = jnp.transpose(unit_own, (1, 2, 3, 0, 4)).reshape(2, per_row, dn * fn * unit_rows).astype(F32)
    back, grad_qup, grad_out, grad_down, grad_gate, grad_up = lax.optimization_barrier(
        (tree_scatter(back_part), grad_qup, grad_out, grad_down, plain(unit_own[0]), plain(unit_own[1]))
    )
    layer_out = (mixed + tree_scatter(after(layer_part, back))).astype(BF)
    grad_qup = jnp.transpose(grad_qup, (2, 1, 3, 0, 4)).reshape(qup_rows, H * HD).astype(F32)

    normed_latent = latent * scale_latent
    latent_back = norm_back(back[:, :latent_width], normed_latent, scale_latent, gain_latent)
    key_grad = rotate(back[:, latent_width : latent_width + HD], own_rows(cosines), -own_rows(sines))
    in_grad = jnp.concatenate([latent_back, key_grad, back[:, latent_width + HD :]], axis=1).astype(BF)

    in_own = other_core(dot_tn(normed_sent, in_grad).astype(BF)).astype(F32) + dot_tn(normed_kept, in_grad)
    in_own = in_own.astype(BF).reshape(dn, zn, per_row, in_width)
    in_parts = exchange(in_own, "dp")
    in_late, back_late, _ = lax.optimization_barrier((in_grad, back, in_own))
    normed_grad = dot_nt(in_late, w_in)
    input_back = norm_back(normed_grad, normed_one, scale_one, gain_one)
    grad_in = (mixed_grad + input_back).astype(BF)
    in_line_parts = jnp.sum(in_parts.astype(F32), axis=0).astype(BF)
    in_sum = total(in_line_parts, LINE)

    gain_cols = gain_column(back_late[:, :latent_width], normed_latent, 2).reshape(dn * fn, per_latent, 128)
    gain_cols = jnp.pad(gain_cols, ((0, 0), (0, per_row - per_latent), (0, 0))).reshape(model, 128)
    gain_cols = gain_cols + gain_two_cols + gain_column(normed_grad, normed_one, 0)
    gain_cols = gain_cols.reshape(dn, zn, cn, per_row, 128)
    gain_own = other_core(at_index(gain_cols, 1 - c_at, 2).astype(BF)).astype(F32) + at_index(gain_cols, c_at, 2)
    gain_own = after(gain_own, in_line_parts)
    gain_sum = at_index(gain_own, d_at)
    for m in range(1, dn):
        gain_sum = gain_sum + over_dp(at_index(gain_own, d_at ^ m).astype(BF), m).astype(F32)
    gain_line, z_at = gain_sum, lax.axis_index(LINE)
    gain_sum = at_index(gain_line, z_at)
    for m in range(1, zn):
        sent = at_index(gain_line, (z_at + m) % zn).astype(BF)
        gain_sum = gain_sum + lax.ppermute(sent, LINE, [(z, (z + m) % zn) for z in range(zn)]).astype(F32)
    return (
        layer_out,
        grad_in,
        gain_sum[:, 0],
        in_sum[:, :latent_width],
        gain_sum[:per_latent, 2],
        grad_qup,
        in_sum[:, latent_width : latent_width + HD],
        in_sum[:, latent_width + HD : in_width],
        grad_out,
        gain_sum[:, 1],
        grad_gate,
        grad_up,
        grad_down,
    )


def solution(mesh):
    dn, fn = mesh.shape["dp"], mesh.shape["fsdp"]
    share = dn * fn // H
    fine = jax.sharding.Mesh(mesh.devices.reshape(dn, fn // share, share // 2, 2), ("dp",) + TREE)
    split = P(("dp",) + TREE, None)
    line = P(("dp",) + TREE)
    placed = (
        split, line, P("dp", None), line, split, line, split, split, split, split, line, split, split, split, split,
    )
    given = (split, split, line, split, line, split, split, split, split, line, split, split, split)
    return jax.shard_map(body, mesh=fine, in_specs=placed, out_specs=given, check_vma=False)
```

```python
import functools

import jax
import jax.numpy as jnp
from jax import lax
from jax.experimental import pallas as pl
from jax.experimental.layout import Layout, with_layout_constraint
from jax.experimental.pallas import tpu as pltpu
from jax.sharding import PartitionSpec as P

H = 16
HD = 256
NSEG = 20

EPSILON = 1e-06
ROPE_BASE = 10000.0
HIGHEST = lax.Precision.HIGHEST
NEGATIVE = -1e30
BF = jnp.bfloat16
F32 = jnp.float32
CHUNK = 320
TREE = ("q", "r", "c")
LINE = ("q", "r")
SHARE = ("r", "c")
VMEM_LIMIT = 56 * 1024 * 1024


def dot32(a, b):
    return jnp.dot(a, b, preferred_element_type=F32)


def dot_nt(a, b):
    return lax.dot_general(a, b, (((1,), (1,)), ((), ())), preferred_element_type=F32)


def dot_tn(a, b):
    return lax.dot_general(a, b, (((0,), (0,)), ((), ())), preferred_element_type=F32)


def rms_scale(values):
    return lax.rsqrt(jnp.mean(values * values, axis=-1, keepdims=True) + EPSILON)


def norm_back(upstream, normed, row_scale, gain_vec):
    scaled = upstream * gain_vec
    inner_mean = jnp.mean(scaled * normed, axis=-1, keepdims=True)
    return row_scale * (scaled - normed * inner_mean)


def gain_column(upstream, normed, column):
    picked = (lax.broadcasted_iota(jnp.int32, (upstream.shape[0], 128), 1) == column).astype(F32)
    return lax.dot_general(
        upstream * normed, picked, (((0,), (0,)), ((), ())), precision=HIGHEST, preferred_element_type=F32
    )


def rotate(values, cosines, sines):
    half = values.shape[-1] // 2
    a, b = values[..., :half], values[..., half:]
    return jnp.concatenate([a * cosines - b * sines, b * cosines + a * sines], axis=-1)


def tile_plan(tile, per_tile):
    free = jnp.minimum(tile, 2) * per_tile
    count = jnp.where(tile == 4, 4, tile + 1) * per_tile
    return free, count


def chunk_start(tile, j, per_tile):
    jump = jnp.where((tile == 4) & (j >= 3 * per_tile), per_tile, 0)
    return pl.multiple_of((j + jump) * CHUNK, CHUNK)


def seen(k0, bits_row, q_pos, seg_len):
    shape = (CHUNK, q_pos.shape[1])
    key_pos = lax.broadcasted_iota(jnp.int32, (CHUNK, 1), 0) + k0
    key_bit = jnp.left_shift(jnp.int32(1), key_pos // seg_len)
    reach = jnp.broadcast_to(key_bit, shape) & jnp.broadcast_to(bits_row, shape)
    return (reach != 0) & (jnp.broadcast_to(key_pos, shape) <= jnp.broadcast_to(q_pos, shape))


def query_places(tile, tile_rows, heads):
    lane = lax.broadcasted_iota(jnp.int32, (1, heads * tile_rows), 1)
    return tile * tile_rows + lax.rem(lane, tile_rows)


def attn_fwd_kernel(heads, seg_len, bits_ref, q_ref, k_ref, v_ref, wo_ref, att_ref, lse_ref, part_ref, qs, st):
    tile_rows = 4 * seg_len
    width = heads * tile_rows
    per_tile = tile_rows // CHUNK
    scale = HD ** (-0.5)

    def one_tile(tile, carry):
        q0 = pl.multiple_of(tile * tile_rows, tile_rows)
        for h in range(heads):
            rows = q_ref[pl.ds(q0, tile_rows), h * HD : (h + 1) * HD]
            qs[h * tile_rows : (h + 1) * tile_rows, :] = (rows.astype(F32) * scale).astype(BF)
        bits_row = bits_ref[tile]
        q_pos = query_places(tile, tile_rows, heads)
        free, count = tile_plan(tile, per_tile)

        def score(masked, j, top):
            k0 = chunk_start(tile, j, per_tile)
            s = dot_nt(k_ref[pl.ds(k0, CHUNK), :], qs[...])
            if masked:
                s = jnp.where(seen(k0, bits_row, q_pos, seg_len), s, NEGATIVE)
            st[pl.ds(pl.multiple_of(j * CHUNK, CHUNK), CHUNK), :] = s
            return jnp.maximum(top, jnp.max(s, axis=0, keepdims=True))

        top = lax.fori_loop(0, free, functools.partial(score, False), jnp.full((1, width), NEGATIVE, F32))
        top = lax.fori_loop(free, count, functools.partial(score, True), top)

        def gather(j, carry):
            total, acc = carry
            k0 = chunk_start(tile, j, per_tile)
            p = jnp.exp(st[pl.ds(pl.multiple_of(j * CHUNK, CHUNK), CHUNK), :] - top)
            acc = acc + dot_tn(v_ref[pl.ds(k0, CHUNK), :], p.astype(BF))
            return total + jnp.sum(p, axis=0, keepdims=True), acc

        total, out = lax.fori_loop(0, count, gather, (jnp.zeros((1, width), F32), jnp.zeros((HD, width), F32)))
        lse_ref[tile] = top + jnp.log(total)
        out = (out * (1.0 / total)).T.astype(BF)
        here = pl.ds(q0, tile_rows)
        part = None
        for h in range(heads):
            cols = slice(h * HD, (h + 1) * HD)
            own = out[h * tile_rows : (h + 1) * tile_rows, :]
            att_ref[here, cols] = own
            more = dot32(own, wo_ref[cols, :])
            part = more if part is None else part + more
        part_ref[here, :] = part.astype(BF)
        return carry

    lax.fori_loop(0, 5, one_tile, 0)


def attn_bwd_kernel(
    heads, seg_len, bits_ref, lse_ref, cos_ref, sin_ref, q_ref, k_ref, v_ref, att_ref, branch_ref, wo_ref, wq_ref,
    dq_ref, back_ref, qs, das, dk, dv,
):
    tile_rows = 4 * seg_len
    width = heads * tile_rows
    per_tile = tile_rows // CHUNK
    scale = HD ** (-0.5)
    dk[...] = jnp.zeros_like(dk)
    dv[...] = jnp.zeros_like(dv)

    def one_tile(tile, carry):
        q0 = pl.multiple_of(tile * tile_rows, tile_rows)
        deltas = []
        for h in range(heads):
            rows = slice(h * tile_rows, (h + 1) * tile_rows)
            cols = slice(h * HD, (h + 1) * HD)
            here = pl.ds(q0, tile_rows)
            qs[rows, :] = (q_ref[here, cols].astype(F32) * scale).astype(BF)
            grad = dot_nt(branch_ref[here, :], wo_ref[cols, :]).astype(BF)
            das[rows, :] = grad
            both = grad.astype(F32) * att_ref[here, cols].astype(F32)
            deltas.append(jnp.sum(both.T, axis=0, keepdims=True))
        delta = jnp.concatenate(deltas, axis=1)
        bits_row = bits_ref[tile]
        lse_row = lse_ref[tile]
        q_pos = query_places(tile, tile_rows, heads)
        free, count = tile_plan(tile, per_tile)

        def step(masked, j, acc):
            k0 = chunk_start(tile, j, per_tile)
            at = pl.ds(k0, CHUNK)
            keys = k_ref[at, :]
            p = jnp.exp(dot_nt(keys, qs[...]) - lse_row)
            if masked:
                p = jnp.where(seen(k0, bits_row, q_pos, seg_len), p, 0.0)
            dp = dot_nt(v_ref[at, :], das[...])
            ds = (p * (dp - delta)).astype(BF)
            dv[at, :] += dot32(p.astype(BF), das[...])
            dk[at, :] += dot32(ds, qs[...])
            return acc + dot_tn(keys, ds)

        acc = lax.fori_loop(0, free, functools.partial(step, False), jnp.zeros((HD, width), F32))
        acc = lax.fori_loop(free, count, functools.partial(step, True), acc)
        out = (acc * scale).T
        at = pl.ds(q0, tile_rows)
        latent = None
        for h in range(heads):
            cols = slice(h * HD, (h + 1) * HD)
            grad = out[h * tile_rows : (h + 1) * tile_rows, :]
            grad = rotate(grad, cos_ref[at, :], -sin_ref[at, :]).astype(BF)
            dq_ref[at, cols] = grad
            more = dot_nt(grad, wq_ref[:, cols])
            latent = more if latent is None else latent + more
        back_ref[at, :latent_width] = latent.astype(BF)
        return carry

    latent_width = wq_ref.shape[0]
    lax.fori_loop(0, 5, one_tile, 0)
    back_ref[:, latent_width : latent_width + HD] = dk[...].astype(BF)
    back_ref[:, latent_width + HD :] = dv[...].astype(BF)


def attention(bits, q, k, v, out_cols, heads, seg_len):
    tree_len = q.shape[0]
    width = heads * 4 * seg_len
    work = heads * tree_len * tree_len // 2
    return pl.pallas_call(
        functools.partial(attn_fwd_kernel, heads, seg_len),
        out_shape=(
            jax.ShapeDtypeStruct((tree_len, heads * HD), BF),
            jax.ShapeDtypeStruct((5, 1, width), F32),
            jax.ShapeDtypeStruct((tree_len, out_cols.shape[1]), BF),
        ),
        in_specs=[pl.BlockSpec(memory_space=pltpu.VMEM)] * 5,
        out_specs=(pl.BlockSpec(memory_space=pltpu.VMEM),) * 3,
        scratch_shapes=[pltpu.VMEM((width, HD), BF), pltpu.VMEM((16 * seg_len, width), F32)],
        compiler_params=pltpu.CompilerParams(vmem_limit_bytes=VMEM_LIMIT),
        cost_estimate=pl.CostEstimate(flops=6 * HD * work, bytes_accessed=6 * tree_len * HD * 2, transcendentals=work),
        name="attn_fwd",
    )(bits, q, k, v, out_cols)


def attention_back(bits, lse, cosines, sines, q, k, v, attended, branch, out_cols, qup_cols, heads, seg_len):
    tree_len = q.shape[0]
    width = heads * 4 * seg_len
    work = heads * tree_len * tree_len // 2
    return pl.pallas_call(
        functools.partial(attn_bwd_kernel, heads, seg_len),
        out_shape=(
            jax.ShapeDtypeStruct((tree_len, heads * HD), BF),
            jax.ShapeDtypeStruct((tree_len, qup_cols.shape[0] + 2 * HD), BF),
        ),
        in_specs=[pl.BlockSpec(memory_space=pltpu.VMEM)] * 11,
        out_specs=(pl.BlockSpec(memory_space=pltpu.VMEM),) * 2,
        scratch_shapes=[
            pltpu.VMEM((width, HD), BF),
            pltpu.VMEM((width, HD), BF),
            pltpu.VMEM((tree_len, HD), F32),
            pltpu.VMEM((tree_len, HD), F32),
        ],
        compiler_params=pltpu.CompilerParams(vmem_limit_bytes=VMEM_LIMIT),
        cost_estimate=pl.CostEstimate(flops=14 * HD * work, bytes_accessed=12 * tree_len * HD * 2, transcendentals=work),
        name="attn_bwd",
    )(bits, lse, cosines, sines, q, k, v, attended, branch, out_cols, qup_cols)


def whole(shape):
    return pl.BlockSpec(shape, lambda i: (0,) * len(shape), pipeline_mode=pl.Buffered(1))


def by_rows(rows, width):
    return pl.BlockSpec((rows, width), lambda i: (i, 0))


def project_kernel(heads, latent_width, x_ref, w_ref, qup_ref, g1_ref, gl_ref, cos_ref, sin_ref, q_ref, k_ref, v_ref, l_ref):
    x = x_ref[...].astype(F32)
    normed = (x * rms_scale(x) * g1_ref[...]).astype(BF)
    latent = dot32(normed, w_ref[:, :latent_width])
    latent_in = (latent * rms_scale(latent) * gl_ref[...]).astype(BF)
    l_ref[...] = latent_in
    cosines, sines = cos_ref[...], sin_ref[...]
    both = dot32(normed, w_ref[:, latent_width : latent_width + 2 * HD])
    k_ref[...] = rotate(both[:, :HD], cosines, sines).astype(BF)
    v_ref[...] = both[:, HD:].astype(BF)
    query = dot32(latent_in, qup_ref[...])
    for h in range(heads):
        at = slice(h * HD, (h + 1) * HD)
        q_ref[:, at] = rotate(query[:, at], cosines, sines).astype(BF)


def project(x, w_in, qup_cols, gain_one, gain_latent, cosines, sines, heads, rows):
    tree_len, model = x.shape
    latent_width = qup_cols.shape[0]
    outs = [(heads * HD, BF), (HD, BF), (HD, BF), (latent_width, BF)]
    flops = 2 * tree_len * (model * (latent_width + 2 * HD) + latent_width * heads * HD)
    return pl.pallas_call(
        functools.partial(project_kernel, heads, latent_width),
        grid=(tree_len // rows,),
        out_shape=[jax.ShapeDtypeStruct((tree_len, w), t) for w, t in outs],
        in_specs=[
            by_rows(rows, model),
            whole(w_in.shape),
            whole(qup_cols.shape),
            whole((1, model)),
            whole((1, latent_width)),
            by_rows(rows, HD // 2),
            by_rows(rows, HD // 2),
        ],
        out_specs=[by_rows(rows, w) for w, _ in outs],
        compiler_params=pltpu.CompilerParams(vmem_limit_bytes=VMEM_LIMIT),
        cost_estimate=pl.CostEstimate(flops=flops, bytes_accessed=tree_len * 10000 + w_in.size * 2, transcendentals=0),
        name="project",
    )(x, w_in, qup_cols, gain_one[None], gain_latent[None], cosines, sines)


def ffn_kernel(mid_ref, cot_ref, wg_ref, wu_ref, wd_ref, act_ref, gg_ref, ug_ref, part_ref):
    mid = mid_ref[...]
    gate = dot32(mid, wg_ref[...])
    up = dot32(mid, wu_ref[...])
    grad = dot_nt(cot_ref[...], wd_ref[...])
    sig = jax.nn.sigmoid(gate)
    silu = gate * sig
    act_ref[...] = (silu * up).astype(BF)
    gate_grad = (grad * up * sig * (1.0 + gate * (1.0 - sig))).astype(BF)
    up_grad = (grad * silu).astype(BF)
    gg_ref[...] = gate_grad
    ug_ref[...] = up_grad
    part_ref[...] = (dot_nt(gate_grad, wg_ref[...]) + dot_nt(up_grad, wu_ref[...])).astype(BF)


def ffn(mid, cot, gate_cols, up_cols, down_rows, rows):
    count, model = mid.shape
    units = gate_cols.shape[1]
    outs = [(units, BF)] * 3 + [(model, BF)]
    return pl.pallas_call(
        ffn_kernel,
        grid=(count // rows,),
        out_shape=[jax.ShapeDtypeStruct((count, w), t) for w, t in outs],
        in_specs=[by_rows(rows, model)] * 2 + [whole(gate_cols.shape)] * 2 + [whole(down_rows.shape)],
        out_specs=[by_rows(rows, w) for w, _ in outs],
        compiler_params=pltpu.CompilerParams(vmem_limit_bytes=VMEM_LIMIT),
        cost_estimate=pl.CostEstimate(
            flops=10 * count * model * units, bytes_accessed=6 * (count + units) * model, transcendentals=count * units
        ),
        name="ffn",
    )(mid, cot, gate_cols, up_cols, down_rows)


def unit_grad_kernel(mid_ref, grad_ref, out_ref, turned):
    @pl.when(pl.program_id(0) == 0)
    def _():
        turned[...] = grad_ref[...].T

    out_ref[0] = dot32(turned[...], mid_ref[...]).astype(BF)


def unit_grads(mid, grad, parts):
    count, model = mid.shape
    units = grad.shape[1]
    wide = model // parts
    return pl.pallas_call(
        unit_grad_kernel,
        grid=(parts,),
        out_shape=jax.ShapeDtypeStruct((parts, units, wide), BF),
        in_specs=[pl.BlockSpec((count, wide), lambda i: (0, i)), whole(grad.shape)],
        out_specs=pl.BlockSpec((1, units, wide), lambda i: (i, 0, 0)),
        scratch_shapes=[pltpu.VMEM((units, count), BF)],
        compiler_params=pltpu.CompilerParams(vmem_limit_bytes=VMEM_LIMIT),
        cost_estimate=pl.CostEstimate(
            flops=2 * count * model * units, bytes_accessed=2 * (count + units) * model, transcendentals=0
        ),
        name="unit_grads",
    )(mid, grad)


def body(
    hidden_in,
    segment_ids,
    parents,
    norm_gain,
    w_qdown,
    q_gain,
    w_qup,
    w_key,
    w_value,
    w_out,
    ffn_gain,
    w_gate,
    w_up,
    w_down,
    cotangent,
):
    rows, model = hidden_in.shape
    dn, cn = lax.axis_size("dp"), lax.axis_size("c")
    zn, sn = lax.axis_size(LINE), lax.axis_size(SHARE)
    fn = lax.axis_size(TREE)
    heads = H // fn
    latent_width = w_qdown.shape[1]
    in_width = latent_width + 2 * HD
    per_row, per_latent = norm_gain.shape[0], q_gain.shape[0]
    d_at, c_at, f_at = lax.axis_index("dp"), lax.axis_index("c"), lax.axis_index(TREE)
    tree_len = rows * fn
    seg_len = tree_len // NSEG
    block_rows = 2 * rows

    def exchange(parts, axes):
        return lax.all_to_all(parts, axes, split_axis=0, concat_axis=0, tiled=True)

    def spread(block, axes):
        return exchange(jnp.broadcast_to(block[None], (lax.axis_size(axes),) + block.shape), axes)

    def total(parts, axes):
        return jnp.sum(exchange(parts.astype(BF), axes).astype(F32), axis=0)

    def other_core(a):
        return lax.ppermute(a, "c", [(c, (c + 1) % cn) for c in range(cn)])

    def by_core(mine, axis):
        came = other_core(mine)
        return jnp.stack([jnp.where(c_at == 0, mine, came), jnp.where(c_at == 0, came, mine)], axis=axis)

    def exchange_share(parts):
        if sn != cn:
            return exchange(parts, SHARE)
        came = other_core(at_index(parts, 1 - c_at))
        return jnp.stack([jnp.where(c_at == 0, parts[0], came), jnp.where(c_at == 0, came, parts[1])])

    def at_index(a, index, axis=0):
        return lax.dynamic_index_in_dim(a, index, axis, keepdims=False)

    def plain(a):
        return with_layout_constraint(a, Layout(major_to_minor=tuple(range(a.ndim))))

    def after(a, *before):
        return lax.optimization_barrier((a,) + before)[0]

    def own_rows(a):
        return lax.dynamic_slice_in_dim(a, f_at * rows, rows, 0)

    def tree_gather(block):
        return lax.all_gather(block, TREE, axis=0, tiled=True)

    def tree_scatter(parts):
        return lax.psum_scatter(parts, TREE, scatter_dimension=0, tiled=True).astype(F32)

    def over_dp(a, m):
        return lax.ppermute(a, "dp", [(d, d ^ m) for d in range(dn)])

    def spread_dp(block):
        out = jnp.zeros((dn,) + block.shape, block.dtype)
        for m in range(dn):
            got = over_dp(block, m) if m else block
            out = lax.dynamic_update_index_in_dim(out, got, d_at ^ m, 0)
        return out

    def spread_line(block):
        out = jnp.zeros((zn,) + block.shape, block.dtype)
        z_at = lax.axis_index(LINE)
        for m in range(zn):
            got = lax.ppermute(block, LINE, [(z, (z + m) % zn) for z in range(zn)]) if m else block
            out = lax.dynamic_update_index_in_dim(out, got, (z_at + zn - m) % zn, 0)
        return out

    tags = -(-rows // per_row)
    extra = jnp.concatenate(
        [
            norm_gain[:, None],
            ffn_gain[:, None],
            jnp.pad(q_gain, (0, per_row - per_latent))[:, None],
            jnp.pad(segment_ids.astype(BF), (0, tags * per_row - rows)).reshape(tags, per_row).T,
            jnp.zeros((per_row, 125 - tags), BF),
        ],
        axis=1,
    )
    x_all = tree_gather(hidden_in)
    in_block = jnp.concatenate([w_qdown, w_key, w_value, extra], axis=1)
    qup_rows, out_rows, unit_rows = w_qup.shape[0], w_out.shape[0], w_down.shape[0]
    qn, units = fn // sn, dn * unit_rows

    def unit_columns(weight):
        return jnp.transpose(weight.reshape(per_row, dn, fn, unit_rows), (2, 0, 1, 3)).reshape(fn, per_row, units)

    unit_sent = jnp.stack([unit_columns(w_gate), unit_columns(w_up)], axis=1)
    qup_cols = jnp.transpose(w_qup.reshape(qup_rows, sn, heads, qn, HD), (3, 1, 0, 2, 4))
    qup_cols = exchange(qup_cols.reshape(fn, qup_rows, heads * HD), TREE)
    out_cols = spread_dp(w_out).reshape(sn, heads, out_rows, model)
    in_line = after(spread_line(in_block), qup_cols, unit_sent, out_cols)
    in_wide = spread(in_line, "dp")
    qup_cols = spread(after(qup_cols, in_wide), "dp").reshape(latent_width, heads * HD)
    in_full = by_core(in_wide, 2).reshape(model, in_width + 128)
    w_in = in_full[:, :in_width]
    extra = in_full[:, in_width:].T.astype(F32)
    gain_one, gain_two = extra[0], extra[1]
    gain_latent = extra[2].reshape(dn * fn, per_row)[:, :per_latent].reshape(latent_width)
    run_labels = lax.dynamic_slice_in_dim(extra[3 : 3 + tags].reshape(tags, dn, fn, per_row), d_at, 1, 1)[:, 0]
    run_labels = jnp.swapaxes(run_labels, 0, 1).reshape(fn, tags * per_row)[:, :rows]
    run_labels = run_labels.reshape(tree_len)[::seg_len].astype(jnp.int32)

    cot = tree_gather(after(cotangent, x_all))

    labels = jnp.arange(NSEG, dtype=jnp.int32)
    reach = jnp.maximum(
        (labels[:, None] == labels[None, :]).astype(F32), (parents[0][:, None] == labels[None, :]).astype(F32)
    )
    for _ in range(5):
        reach = jnp.minimum(jnp.dot(reach, reach, precision=HIGHEST), 1.0)
    pick_run = (run_labels[:, None] == labels[None, :]).astype(F32)
    run_reach = jnp.dot(jnp.dot(pick_run, reach, precision=HIGHEST), pick_run.T, precision=HIGHEST)
    run_depth = jnp.sum(run_reach, axis=1) - 1.0
    run_bits = jnp.sum(jnp.where(run_reach > 0.5, jnp.left_shift(1, labels)[None, :], 0), axis=1).astype(jnp.int32)
    bits = jnp.broadcast_to(run_bits.reshape(5, 1, 4, 1), (5, heads, 4, seg_len)).reshape(5, 1, heads * 4 * seg_len)
    inverse = ROPE_BASE ** (-(jnp.arange(HD // 2, dtype=F32) * 2.0) / HD)
    coarse = (run_depth * seg_len)[:, None] * inverse[None, :]
    fine = jnp.arange(seg_len, dtype=F32)[:, None] * inverse[None, :]
    cos_a, sin_a = jnp.cos(coarse)[:, None, :], jnp.sin(coarse)[:, None, :]
    cos_b, sin_b = jnp.cos(fine)[None, :, :], jnp.sin(fine)[None, :, :]
    cosines = (cos_a * cos_b - sin_a * sin_b).reshape(tree_len, HD // 2)
    sines = (sin_a * cos_b + cos_a * sin_b).reshape(tree_len, HD // 2)

    query_all, key_all, value_all, latent_in = project(
        x_all, in_full, qup_cols, gain_one, gain_latent, cosines, sines, heads, block_rows
    )
    unit_cols = exchange(after(unit_sent, x_all, qup_cols), TREE)
    out_cols = jnp.swapaxes(exchange_share(after(out_cols, key_all)), 0, 1).reshape(heads * HD, model)
    attended, lse, out_part = attention(bits, query_all, key_all, value_all, out_cols, heads, seg_len)
    x = hidden_in.astype(F32)
    down_sent = after(w_down, x_all)
    down_got = [over_dp(down_sent, m) for m in range(1, dn)]
    out_part, _, _, *down_got = lax.optimization_barrier((out_part, cot, unit_cols, *down_got))
    gate_cols = spread(unit_cols[:, 0], "dp").reshape(model, units)
    up_cols = spread(after(unit_cols[:, 1], out_part), "dp").reshape(model, units)
    scale_one = rms_scale(x)
    normed_one = x * scale_one
    normed_in = (normed_one * gain_one).astype(BF)
    latent = dot32(after(normed_in, out_part), w_in[:, :latent_width])
    scale_latent = rms_scale(latent)

    def per_core(a, core):
        return at_index(a.reshape(a.shape[0], dn * zn, cn, per_row), core, 2).reshape(a.shape[0], dn * zn * per_row)

    normed_kept, normed_sent = per_core(normed_in, c_at), per_core(normed_in, 1 - c_at)
    down_rows = jnp.zeros((dn, unit_rows, model), BF)
    for m, got in enumerate([after(w_down, out_part)] + down_got):
        down_rows = lax.dynamic_update_index_in_dim(down_rows, got, d_at ^ m, 0)
    down_rows = down_rows.reshape(units, model)
    mixed = x + after(tree_scatter(out_part), gate_cols, down_rows, scale_latent, normed_kept, normed_sent)
    mixed = lax.optimization_barrier(mixed)

    scale_two = rms_scale(mixed)
    normed_two = mixed * scale_two
    normed_mid = (normed_two * gain_two).astype(BF)
    mid = after(tree_gather(normed_mid), down_rows, gate_cols, up_cols)
    activated, gate_grad, up_grad, mid_part = ffn(mid, cot, gate_cols, up_cols, down_rows, block_rows)
    gate_parts = unit_grads(after(mid, mid_part), gate_grad, dn)
    down_parts = dot_tn(after(activated, gate_parts), cot).astype(BF).reshape(dn, unit_rows, model)
    up_parts = unit_grads(after(mid, down_parts), up_grad, dn)
    gate_parts = exchange(gate_parts, "dp")
    mid_grad = after(tree_scatter(mid_part), gate_parts, down_parts, up_parts)
    up_parts = exchange(after(up_parts, gate_parts), "dp")
    layer_part = dot32(after(activated, up_grad), down_rows).astype(BF)
    mixed_back = norm_back(mid_grad, normed_two, scale_two, gain_two)
    gain_two_cols = gain_column(mid_grad, normed_two, 1)
    mixed_grad = lax.optimization_barrier(cotangent.astype(F32) + mixed_back)
    branch_grad = mixed_grad.astype(BF)


    def unit_sum(parts):
        return jnp.sum(parts.astype(F32), axis=0).astype(BF).reshape(units, fn, per_row)

    unit_own = jnp.stack([unit_sum(gate_parts), unit_sum(up_parts)])
    unit_own = plain(jnp.transpose(unit_own, (2, 0, 3, 1)))
    down_sent = [at_index(down_parts, d_at ^ m) for m in range(dn)]
    branch, layer_part, gain_two_cols, unit_own, *down_sent = lax.optimization_barrier(
        (tree_gather(branch_grad), layer_part, gain_two_cols, unit_own, *down_sent)
    )
    down_got = [over_dp(down_sent[m], m) for m in range(1, dn)]
    unit_got = exchange(unit_own, TREE)
    query_grad, back_part = attention_back(
        bits, lse, cosines, sines, query_all, key_all, value_all, attended, branch, out_cols, qup_cols, heads, seg_len
    )
    back_part, unit_got, *down_got = lax.optimization_barrier((back_part, unit_got, *down_got))
    grad_down = down_sent[0].astype(F32)
    for got in down_got:
        grad_down = grad_down + got.astype(F32)
    out_grads = jnp.swapaxes(
        dot_tn(attended, after(branch, back_part)).astype(BF).reshape(heads, sn, out_rows, model), 0, 1
    )
    out_grads = exchange_share(out_grads).reshape(dn, out_rows, model)
    grad_out = at_index(out_grads, d_at).astype(F32)
    for m in range(1, dn):
        grad_out = grad_out + over_dp(at_index(out_grads, d_at ^ m), m).astype(F32)
    grad_qup = dot_tn(latent_in, after(query_grad, back_part, out_grads))
    grad_qup = total(grad_qup.reshape(dn, fn * qup_rows, heads * HD), "dp").astype(BF)
    grad_qup = exchange(grad_qup.reshape(fn, qup_rows, heads * HD), TREE).reshape(qn, sn, qup_rows, heads, HD)
    unit_own = after(unit_got, out_grads).reshape(fn, 2, per_row, dn, unit_rows)
    unit_own = jnp.transpose(unit_own, (1, 2, 3, 0, 4)).reshape(2, per_row, dn * fn * unit_rows).astype(F32)
    back, grad_qup, grad_out, grad_down, grad_gate, grad_up = lax.optimization_barrier(
        (tree_scatter(back_part), grad_qup, grad_out, grad_down, plain(unit_own[0]), plain(unit_own[1]))
    )
    layer_out = (mixed + tree_scatter(after(layer_part, back))).astype(BF)
    grad_qup = jnp.transpose(grad_qup, (2, 1, 3, 0, 4)).reshape(qup_rows, H * HD).astype(F32)

    normed_latent = latent * scale_latent
    latent_back = norm_back(back[:, :latent_width], normed_latent, scale_latent, gain_latent)
    key_grad = rotate(back[:, latent_width : latent_width + HD], own_rows(cosines), -own_rows(sines))
    in_grad = jnp.concatenate([latent_back, key_grad, back[:, latent_width + HD :]], axis=1).astype(BF)

    in_own = other_core(dot_tn(normed_sent, in_grad).astype(BF)).astype(F32) + dot_tn(normed_kept, in_grad)
    in_own = in_own.astype(BF).reshape(dn, zn, per_row, in_width)
    in_parts = exchange(in_own, "dp")
    in_late, back_late, _ = lax.optimization_barrier((in_grad, back, in_own))
    normed_grad = dot_nt(in_late, w_in)
    input_back = norm_back(normed_grad, normed_one, scale_one, gain_one)
    grad_in = (mixed_grad + input_back).astype(BF)
    in_line_parts = jnp.sum(in_parts.astype(F32), axis=0).astype(BF)
    in_sum = total(in_line_parts, LINE)

    gain_cols = gain_column(back_late[:, :latent_width], normed_latent, 2).reshape(dn * fn, per_latent, 128)
    gain_cols = jnp.pad(gain_cols, ((0, 0), (0, per_row - per_latent), (0, 0))).reshape(model, 128)
    gain_cols = gain_cols + gain_two_cols + gain_column(normed_grad, normed_one, 0)
    gain_cols = gain_cols.reshape(dn, zn, cn, per_row, 128)
    gain_own = other_core(at_index(gain_cols, 1 - c_at, 2).astype(BF)).astype(F32) + at_index(gain_cols, c_at, 2)
    gain_own = after(gain_own, in_line_parts)
    gain_sum = at_index(gain_own, d_at)
    for m in range(1, dn):
        gain_sum = gain_sum + over_dp(at_index(gain_own, d_at ^ m).astype(BF), m).astype(F32)
    gain_line, z_at = gain_sum, lax.axis_index(LINE)
    gain_sum = at_index(gain_line, z_at)
    for m in range(1, zn):
        sent = at_index(gain_line, (z_at + m) % zn).astype(BF)
        gain_sum = gain_sum + lax.ppermute(sent, LINE, [(z, (z + m) % zn) for z in range(zn)]).astype(F32)
    return (
        layer_out,
        grad_in,
        gain_sum[:, 0],
        in_sum[:, :latent_width],
        gain_sum[:per_latent, 2],
        grad_qup,
        in_sum[:, latent_width : latent_width + HD],
        in_sum[:, latent_width + HD : in_width],
        grad_out,
        gain_sum[:, 1],
        grad_gate,
        grad_up,
        grad_down,
    )


def solution(mesh):
    dn, fn = mesh.shape["dp"], mesh.shape["fsdp"]
    share = dn * fn // H
    fine = jax.sharding.Mesh(mesh.devices.reshape(dn, fn // share, share // 2, 2), ("dp",) + TREE)
    split = P(("dp",) + TREE, None)
    line = P(("dp",) + TREE)
    placed = (
        split, line, P("dp", None), line, split, line, split, split, split, split, line, split, split, split, split,
    )
    given = (split, split, line, split, line, split, split, split, split, line, split, split, split)
    return jax.shard_map(body, mesh=fine, in_specs=placed, out_specs=given, check_vma=False)
```
